32 devices in a mesh: dp: 2 (over core), gx: 4 (over z), gy: 4 (over y, x).
Axes of the slice: x: 2, y: 2, z: 4, core: 2. Of those that a mesh axis runs over, the one named last changes fastest.
Arguments:
- latents_in: bfloat16 [16384, 1152], P(('dp', 'gy', 'gx')), may hold values from -6 to 6
- condition: bfloat16 [16, 1152], P('dp', 'gy'), may hold values from -6 to 6
- ada_weight: bfloat16 [1152, 6, 1152], P('gy'), may hold values from -0.1875 to 0.1875
- ada_bias: float32 [6, 1152], replicated, may hold values from -1.75 to 1.75
- query_weight: bfloat16 [1152, 1152], P('gx', 'gy'), may hold values from -1 to 1
- key_weight: bfloat16 [1152, 1152], P('gx', 'gy'), may hold values from -0.1875 to 0.1875
- value_weight: bfloat16 [1152, 1152], P('gx', 'gy'), may hold values from -0.1875 to 0.1875
- query_bias: float32 [1152], P('gy'), may hold values from -1.75 to 1.75
- value_bias: float32 [1152], P('gy'), may hold values from -1.75 to 1.75
- out_weight: bfloat16 [1152, 1152], P('gy', 'gx'), may hold values from -0.75 to 0.75
- out_bias: float32 [1152], P('gx'), may hold values from -1.75 to 1.75
- up_weight: bfloat16 [1152, 4608], P('gx', 'gy'), may hold values from -0.1875 to 0.1875
- up_bias: float32 [4608], P('gy'), may hold values from -1.75 to 1.75
- down_weight: bfloat16 [4608, 1152], P('gy', 'gx'), may hold values from -0.09375 to 0.09375
- down_bias: float32 [1152], P('gx'), may hold values from -1.75 to 1.75
- grad_out: float32 [16384, 1152], P(('dp', 'gy', 'gx')), may hold values from -6 to 6
Outputs:
- latents_out: float32 [16384, 1152], P(('dp', 'gy', 'gx'))
- grad_latents: float32 [16384, 1152], P(('dp', 'gy', 'gx'))
- grad_condition: float32 [16, 1152], P('dp', 'gy')
- grad_ada_weight: float32 [1152, 6, 1152], P('gy')
- grad_ada_bias: float32 [6, 1152], replicated
- grad_query_weight: float32 [1152, 1152], P('gx', 'gy')
- grad_key_weight: float32 [1152, 1152], P('gx', 'gy')
- grad_value_weight: float32 [1152, 1152], P('gx', 'gy')
- grad_query_bias: float32 [1152], P('gy')
- grad_value_bias: float32 [1152], P('gy')
- grad_out_weight: float32 [1152, 1152], P('gy', 'gx')
- grad_out_bias: float32 [1152], P('gx')
- grad_up_weight: float32 [1152, 4608], P('gx', 'gy')
- grad_up_bias: float32 [4608], P('gy')
- grad_down_weight: float32 [4608, 1152], P('gy', 'gx')
- grad_down_bias: float32 [1152], P('gx')
- logit_max: float32 [16], P('gy')
- clipped_query_weight: float32 [1152, 1152], P('gx', 'gy')
- clipped_key_weight: float32 [1152, 1152], P('gx', 'gy')
- clipped_query_bias: float32 [1152], P('gy')
The draws below stay inside these ranges and needn't reach their ends.
All inputs are finite; a program needn't handle non-finite values.
Results may differ from the reference program's by a relative error of at most 0.0169.
Values may be sent and summed in bfloat16 or wider, within the bound.
No kernel may reach another device: no remote copies, remote signals or barrier semaphores. Data moves between devices by JAX's collectives and lax.ppermute only.
A program may use at most 256 MiB of HBM per device.

```python
import math
import jax
import jax.numpy as jnp
from jax import lax

D = 1152
HEADS = 16
HD = 72
FF = 4608
SEQ = 1024
TAU = 8
LATENTS = 16
TOKENS = 16384


def draw_query_weight(key, part):
    head_scale = jnp.exp(jax.random.uniform(jax.random.fold_in(key, 11), (HEADS,), jnp.float32, jnp.log(0.7), jnp.log(2.0)))
    column_scale = jnp.repeat(head_scale, HD)
    entries = jnp.clip(jax.random.normal(jax.random.fold_in(key, 12), (D, D), jnp.float32), -4.0, 4.0)
    return (entries * column_scale[None, :] * D ** (-0.5)).astype(jnp.bfloat16)


def shard_levels(rng, dims, shards, smallest, top_value):
    gain = 1.0
    for position, blocks in shards:
        steps = jax.random.uniform(jax.random.fold_in(jax.random.fold_in(rng, 6), position), (blocks,), jnp.float32, smallest / len(shards), top_value / len(shards))
        gain = gain * jnp.repeat(jnp.exp(steps), dims[position] // blocks).reshape((-1,) + (1,) * (len(dims) - 1 - position))
    return gain


def normal_values(stream_key, dims, spread, limit, cuts=(), kind=jnp.bfloat16):
    factor_of = shard_levels(stream_key, dims, cuts, -0.22, 0.18) if cuts else 1.0
    result = jax.random.normal(stream_key, dims, jnp.float32) * spread * factor_of
    return jnp.minimum(jnp.maximum(result, -limit), limit).astype(kind)


def setup_inputs(seed: int = 0) -> dict:
    keys = jax.random.split(jax.random.key(seed), 17)
    latents_in = normal_values(keys[0], (TOKENS, D), 1.0, 6.0, ((0, 32),))
    condition = normal_values(keys[1], (LATENTS, D), 1.0, 6.0, ((0, 2), (1, 4)))
    ada_weight = normal_values(keys[2], (D, 6, D), D ** -0.5, 0.1875, ((0, 4),))
    ada_bias = normal_values(keys[3], (6, D), 0.3, 1.75, (), jnp.float32)
    query_weight = draw_query_weight(jax.random.fold_in(keys[16], 71), 0)
    key_weight = normal_values(keys[5], (D, D), D ** -0.5, 0.1875, ((0, 4), (1, 4)))
    value_weight = normal_values(keys[6], (D, D), D ** -0.5, 0.1875, ((0, 4), (1, 4)))
    query_bias = normal_values(keys[7], (D,), 0.3, 1.75, ((0, 4),), jnp.float32)
    value_bias = normal_values(keys[8], (D,), 0.3, 1.75, ((0, 4),), jnp.float32)
    out_weight = normal_values(keys[9], (D, D), (D // 16) ** -0.5, 0.75, ((0, 4), (1, 4)))
    out_bias = normal_values(keys[10], (D,), 0.3, 1.75, ((0, 4),), jnp.float32)
    up_weight = normal_values(keys[11], (D, FF), D ** -0.5, 0.1875, ((0, 4), (1, 4)))
    up_bias = normal_values(keys[12], (FF,), 0.3, 1.75, ((0, 4),), jnp.float32)
    down_weight = normal_values(keys[13], (FF, D), FF ** -0.5, 0.09375, ((0, 4), (1, 4)))
    down_bias = normal_values(keys[14], (D,), 0.3, 1.75, ((0, 4),), jnp.float32)
    grad_out = normal_values(keys[15], (TOKENS, D), 1.0, 6.0, ((0, 32),), jnp.float32)
    return {"latents_in": latents_in, "condition": condition, "ada_weight": ada_weight, "ada_bias": ada_bias, "query_weight": query_weight, "key_weight": key_weight, "value_weight": value_weight, "query_bias": query_bias, "value_bias": value_bias, "out_weight": out_weight, "out_bias": out_bias, "up_weight": up_weight, "up_bias": up_bias, "down_weight": down_weight, "down_bias": down_bias, "grad_out": grad_out}


@jax.custom_vjp
def low(v):
    return lax.optimization_barrier(v.astype(jnp.bfloat16)).astype(jnp.float32)

@jax.custom_vjp
def low_back(v):
    return v

def low_keep(v):
    return (low(v), None)

def low_pass(kept, grad):
    return (grad,)

def back_keep(v):
    return (v, None)

def back_low(kept, grad):
    return (low(grad),)
low.defvjp(low_keep, low_pass)
low_back.defvjp(back_keep, back_low)
HIGH = lax.Precision.HIGHEST
EPS = 1e-06
GELU_ROOT = 0.7978845608028654
GELU_CUBE = 0.044715

def gelu_tanh(inputs):
    return 0.5 * inputs * (1.0 + jnp.tanh(GELU_ROOT * (inputs + GELU_CUBE * inputs * inputs * inputs)))

def layer_norm(rows_in):
    mean_row = lax.optimization_barrier(jnp.mean(rows_in, axis=-1, keepdims=True))
    centred = rows_in - mean_row
    spread_row = lax.optimization_barrier(jnp.mean(centred * centred, axis=-1, keepdims=True))
    return centred * lax.rsqrt(spread_row + EPS)

def attend(queries, keys_in, values_in):
    scores = jnp.einsum('qhd,khd->hqk', queries, keys_in, precision=HIGH) * (1.0 / math.sqrt(HD))
    scores = low_back(scores)
    head_top = lax.optimization_barrier(jnp.max(scores, axis=(1, 2)))
    probs_low = low(jax.nn.softmax(scores, axis=-1))
    mixed_rows = jnp.einsum('hqk,khd->qhd', probs_low, values_in, precision=HIGH)
    return (mixed_rows, head_top)

def attend_packed(packed):
    return jax.checkpoint(attend)(packed[0], packed[1], packed[2])

def forward(params, latents, cond_rows):
    ada_w, ada_b, query_w, key_w, value_w, query_b, value_b, out_w, out_b, up_w, up_b, down_w, down_b = params
    group_size = cond_rows.shape[0]
    silu_low = low(jax.nn.silu(cond_rows))
    modulation = jnp.einsum('le,emf->lmf', silu_low, ada_w, precision=HIGH) + ada_b
    mod_parts = [modulation[:, column][:, None, :] for column in range(6)]
    shaped = latents.reshape(group_size, SEQ, D)
    hidden_one = low(layer_norm(shaped) * (1.0 + mod_parts[1]) + mod_parts[0]).reshape(group_size * SEQ, D)
    queries = low(low_back(jnp.dot(hidden_one, query_w, precision=HIGH)) + query_b)
    keys_all = low(low_back(jnp.dot(hidden_one, key_w, precision=HIGH)))
    values_all = low(low_back(jnp.dot(hidden_one, value_w, precision=HIGH)) + value_b)
    heads_shape = (group_size, SEQ, HEADS, HD)
    mixed_all, head_tops = lax.map(attend_packed, (queries.reshape(heads_shape), keys_all.reshape(heads_shape), values_all.reshape(heads_shape)))
    mixed_low = low(low_back(mixed_all.reshape(group_size * SEQ, D)))
    attn_out = low_back(jnp.dot(mixed_low, out_w, precision=HIGH)) + out_b
    after_attn = shaped + mod_parts[2] * attn_out.reshape(group_size, SEQ, D)
    hidden_two = low(layer_norm(after_attn) * (1.0 + mod_parts[4]) + mod_parts[3]).reshape(group_size * SEQ, D)
    up_pre = low_back(jnp.dot(hidden_two, up_w, precision=HIGH)) + up_b
    activation = low(gelu_tanh(up_pre))
    mlp_out = low_back(jnp.dot(activation, down_w, precision=HIGH)) + down_b
    block_out = after_attn + mod_parts[5] * mlp_out.reshape(group_size, SEQ, D)
    return (block_out.reshape(group_size * SEQ, D), lax.optimization_barrier(jnp.max(head_tops, axis=0)))

def reference(latents_in, condition, ada_weight, ada_bias, query_weight, key_weight, value_weight, query_bias, value_bias, out_weight, out_bias, up_weight, up_bias, down_weight, down_bias, grad_out):
    params = tuple((entry.astype(jnp.float32) for entry in (ada_weight, ada_bias, query_weight, key_weight, value_weight, query_bias, value_bias, out_weight, out_bias, up_weight, up_bias, down_weight, down_bias)))
    group_size = math.gcd(LATENTS, max(1, 4096 // SEQ))
    steps_count = LATENTS // group_size
    latents_all = latents_in.astype(jnp.float32).reshape(steps_count, group_size * SEQ, D)
    cond_all = condition.astype(jnp.float32).reshape(steps_count, group_size, D)
    cotangents = grad_out.astype(jnp.float32).reshape(steps_count, group_size * SEQ, D)

    def advance(carry, packed_in):
        grad_totals, top_logits = carry
        latents, cond_rows, cotangent = packed_in
        block_out, pullback, head_top = jax.vjp(forward, params, latents, cond_rows, has_aux=True)
        grad_params, grad_latents, grad_cond = pullback(cotangent)
        grad_totals = jax.tree.map(jnp.add, grad_totals, grad_params)
        return ((grad_totals, jnp.maximum(top_logits, head_top)), (block_out, grad_latents, grad_cond))
    initial = (jax.tree.map(jnp.zeros_like, params), jnp.full((HEADS,), -1e+30, dtype=jnp.float32))
    (grad_totals, top_logits), (outs_all, grad_lat_all, grad_cond_all) = lax.scan(advance, initial, (latents_all, cond_all, cotangents))
    factor = TAU / jnp.maximum(top_logits, TAU)
    root_factor = jnp.sqrt(factor)
    clipped_query = (params[2].reshape(D, HEADS, HD) * root_factor[None, :, None]).reshape(D, D)
    clipped_key = (params[3].reshape(D, HEADS, HD) * root_factor[None, :, None]).reshape(D, D)
    clipped_bias = (params[5].reshape(HEADS, HD) * root_factor[:, None]).reshape(D)
    return (outs_all.reshape(TOKENS, D), grad_lat_all.reshape(TOKENS, D), grad_cond_all.reshape(LATENTS, D), grad_totals[0], grad_totals[1], grad_totals[2], grad_totals[3], grad_totals[4], grad_totals[5], grad_totals[6], grad_totals[7], grad_totals[8], grad_totals[9], grad_totals[10], grad_totals[11], grad_totals[12], top_logits, clipped_query, clipped_key, clipped_bias)
```

```python
import math

import jax
import jax.numpy as jnp
from jax import lax
from jax.sharding import PartitionSpec as P

HD = 72
SEQ = 1024
TAU = 8

EPS = 1e-06
GELU_ROOT = 0.7978845608028654
GELU_CUBE = 0.044715
BF = jnp.bfloat16
F32 = jnp.float32
EVERY = ("gy", "gx", "dp")


def gelu_parts(inputs):
    inner_arg = GELU_ROOT * (inputs + GELU_CUBE * inputs * inputs * inputs)
    tangent = jnp.tanh(inner_arg)
    output = 0.5 * inputs * (1.0 + tangent)
    slope_rows = 0.5 * (1.0 + tangent) + 0.5 * inputs * (1.0 - tangent * tangent) * GELU_ROOT * (
        1.0 + 3.0 * GELU_CUBE * inputs * inputs
    )
    return (output, slope_rows)


def normalize(rows_in):
    mean_row = jnp.mean(rows_in, axis=1, keepdims=True)
    centred = rows_in - mean_row
    inverse = lax.rsqrt(jnp.mean(centred * centred, axis=1, keepdims=True) + EPS)
    return (centred * inverse, inverse)


def normalize_back(grad_hat, normed, inverse):
    grad_mean = jnp.mean(grad_hat, axis=1, keepdims=True)
    cross_mean = jnp.mean(grad_hat * normed, axis=1, keepdims=True)
    return inverse * (grad_hat - grad_mean - normed * cross_mean)


def gather_weight(shard):
    part = shard.shape[0] // lax.axis_size("dp")
    mine = lax.dynamic_slice_in_dim(shard, lax.axis_index("dp") * part, part, 0)
    full = lax.all_gather(mine, EVERY, axis=0, tiled=True)
    return full.reshape(lax.axis_size("gy"), -1, shard.shape[1])


def scatter_grad(blocks):
    flat = blocks.reshape(-1, blocks.shape[2])
    mine = lax.psum_scatter(flat, EVERY, scatter_dimension=0, tiled=True)
    return lax.all_gather(mine, "dp", axis=0, tiled=True).astype(F32)


def dot(spec, left, right):
    return jnp.einsum(spec, left, right, preferred_element_type=F32)


def attend_group(packed):
    queries, keys_in, values_in = packed
    scores = dot("qhd,khd->hqk", queries, keys_in) * (1.0 / math.sqrt(HD))
    top_row = jnp.max(scores, axis=2)
    weights = jnp.exp(scores - top_row[:, :, None])
    denominator = jnp.sum(weights, axis=2)
    prob_rows = (weights / denominator[:, :, None]).astype(BF)
    mixed_rows = dot("hqk,khd->qhd", prob_rows, values_in)
    return (mixed_rows.astype(BF), top_row + jnp.log(denominator), jnp.max(top_row, axis=1))


def attend_back(packed):
    queries, keys_in, values_in, grad_mixed, log_sums = packed
    scores = dot("qhd,khd->hqk", queries, keys_in) * (1.0 / math.sqrt(HD))
    prob_rows = jnp.exp(scores - log_sums[:, :, None])
    prob_low = prob_rows.astype(BF)
    grad_probs = dot("qhd,khd->hqk", grad_mixed, values_in)
    row_delta = jnp.sum(grad_probs * prob_rows, axis=2)
    grad_scores = (prob_rows * (grad_probs - row_delta[:, :, None])).astype(BF)
    grad_query = dot("hqk,khd->qhd", grad_scores, keys_in) * (1.0 / math.sqrt(HD))
    grad_key = dot("hqk,qhd->khd", grad_scores, queries) * (1.0 / math.sqrt(HD))
    grad_value = dot("hqk,qhd->khd", prob_low, grad_mixed)
    return (grad_query, grad_key, grad_value)


def body(
    latents_in,
    condition,
    ada_weight,
    ada_bias,
    query_weight,
    key_weight,
    value_weight,
    query_bias,
    value_bias,
    out_weight,
    out_bias,
    up_weight,
    up_bias,
    down_weight,
    down_bias,
    grad_out,
):
    rows, width = latents_in.shape
    latent_count = condition.shape[0]
    cols = query_weight.shape[1]
    width_x = out_bias.shape[0]
    size_gx, size_gy = lax.axis_size("gx"), lax.axis_size("gy")
    at_gx, at_gy = lax.axis_index("gx"), lax.axis_index("gy")
    span = SEQ // rows
    heads_here = cols // HD

    def shift_pairs(shift):
        return [(i, i // span * span + (i + shift) % span) for i in range(size_gx)]

    context = jnp.concatenate(
        [latents_in] + [lax.ppermute(latents_in, "gx", shift_pairs(s)) for s in range(1, span)], axis=0
    )

    cond_f32 = condition.astype(F32)
    silu_cond = jax.nn.silu(cond_f32).astype(BF)
    mod_part = dot("le,emf->lmf", silu_cond, ada_weight)
    mod_group = lax.psum_scatter(mod_part, "gy", scatter_dimension=0, tiled=True)
    mod_own = lax.dynamic_index_in_dim(mod_group, at_gx // span, 0, keepdims=False) + ada_bias
    shift_one, scale_one, gate_one, shift_two, scale_two, gate_two = [
        mod_own[m : m + 1] for m in range(6)
    ]

    wide = lax.all_gather(
        jnp.concatenate([out_bias, down_bias, query_bias, value_bias, up_bias])[None],
        ("gy", "gx"),
        axis=0,
        tiled=True,
    )
    out_bias_all = wide[:size_gx, :width_x].reshape(1, width)
    down_bias_all = wide[:size_gx, width_x : 2 * width_x].reshape(1, width)
    rest = wide[::size_gx, 2 * width_x :]
    query_bias_all = rest[:, None, :cols]
    value_bias_all = rest[:, None, cols : 2 * cols]
    up_bias_all = rest[:, None, 2 * cols :]

    attn_w = gather_weight(
        jnp.concatenate([query_weight, key_weight, value_weight, out_weight.T], axis=1)
    )
    up_w = gather_weight(up_weight)
    down_w = gather_weight(down_weight.T)
    query_w, key_w, value_w, out_w = [attn_w[:, :, i * cols : (i + 1) * cols] for i in range(4)]

    normed_ctx, inverse_ctx = normalize(context.astype(F32))
    hidden_ctx = (normed_ctx * (1.0 + scale_one) + shift_one).astype(BF)
    normed_one, inverse_one, hidden_one = normed_ctx[:rows], inverse_ctx[:rows], hidden_ctx[:rows]
    residual = latents_in.astype(F32)
    queries = (dot("rd,gdn->grn", hidden_one, query_w) + query_bias_all).astype(BF)
    keys_ctx = dot("rd,gdn->grn", hidden_ctx, key_w).astype(BF)
    values_ctx = (dot("rd,gdn->grn", hidden_ctx, value_w) + value_bias_all).astype(BF)

    def split_heads(matrix_rows):
        return matrix_rows.reshape(size_gy, -1, heads_here, HD)

    mixed, log_sums, head_tops = lax.map(
        attend_group, (split_heads(queries), split_heads(keys_ctx), split_heads(values_ctx))
    )
    mixed = mixed.reshape(size_gy, rows, cols)
    top_all = lax.pmax(head_tops.reshape(-1), ("dp", "gx", "gy"))
    logit_max = lax.dynamic_slice_in_dim(top_all, at_gy * heads_here, heads_here, 0)

    attn_out = dot("grn,gdn->rd", mixed, out_w) + out_bias_all
    after_attn = residual + gate_one * attn_out
    normed_two, inverse_two = normalize(after_attn)
    hidden_two = (normed_two * (1.0 + scale_two) + shift_two).astype(BF)
    up_pre = dot("rd,gdn->grn", hidden_two, up_w) + up_bias_all
    activ_f32, gelu_slope = gelu_parts(up_pre)
    activation = activ_f32.astype(BF)
    mlp_out = dot("grn,gdn->rd", activation, down_w) + down_bias_all
    block_out = after_attn + gate_two * mlp_out

    grad_mlp = gate_two * grad_out
    grad_mlp_low = grad_mlp.astype(BF)
    grad_act = dot("rd,gdn->grn", grad_mlp_low, down_w)
    grad_down_w = scatter_grad(dot("rd,grn->gdn", grad_mlp_low, activation).astype(BF))
    grad_up_pre = grad_act * gelu_slope
    grad_up_low = grad_up_pre.astype(BF)
    grad_hidden_two = dot("grn,gdn->rd", grad_up_low, up_w)
    grad_up_w = scatter_grad(dot("rd,grn->gdn", hidden_two, grad_up_low).astype(BF))
    grad_after = grad_out + normalize_back(
        grad_hidden_two * (1.0 + scale_two), normed_two, inverse_two
    )
    grad_attn = gate_one * grad_after
    grad_attn_low = grad_attn.astype(BF)
    grad_mixed_low = dot("rd,gdn->grn", grad_attn_low, out_w).astype(BF)
    grad_out_w = dot("rd,grn->gdn", grad_attn_low, mixed).astype(BF)
    grad_query, grad_key, grad_value = lax.map(
        attend_back,
        (
            split_heads(queries),
            split_heads(keys_ctx),
            split_heads(values_ctx),
            split_heads(grad_mixed_low),
            log_sums,
        ),
    )
    grad_query = grad_query.reshape(size_gy, rows, cols)
    grad_value = grad_value.reshape(size_gy, SEQ, cols)
    grad_query_low = grad_query.astype(BF)
    grad_key_low = grad_key.reshape(size_gy, SEQ, cols).astype(BF)
    grad_value_low = grad_value.astype(BF)
    grad_ctx = dot("grn,gdn->rd", grad_key_low, key_w) + dot("grn,gdn->rd", grad_value_low, value_w)
    grad_hidden_one = grad_ctx[:rows] + dot("grn,gdn->rd", grad_query_low, query_w)
    for s in range(1, span):
        back = [(b, a) for a, b in shift_pairs(s)]
        grad_hidden_one += lax.ppermute(
            grad_ctx[s * rows : (s + 1) * rows].astype(BF), "gx", back
        ).astype(F32)
    grad_attn_w = scatter_grad(
        jnp.concatenate(
            [
                dot("rd,grn->gdn", hidden_one, grad_query_low).astype(BF),
                dot("rd,grn->gdn", hidden_ctx, grad_key_low).astype(BF),
                dot("rd,grn->gdn", hidden_ctx, grad_value_low).astype(BF),
                grad_out_w,
            ],
            axis=2,
        )
    )
    grad_input = grad_after + normalize_back(
        grad_hidden_one * (1.0 + scale_one), normed_one, inverse_one
    )

    def rows_sum(values):
        return jnp.sum(values, axis=-2).reshape(-1, width)

    tail_part = jnp.concatenate(
        [
            rows_sum(grad_hidden_one),
            rows_sum(grad_hidden_one * normed_one),
            rows_sum(grad_after * attn_out),
            rows_sum(grad_hidden_two),
            rows_sum(grad_hidden_two * normed_two),
            rows_sum(grad_out * mlp_out),
            rows_sum(grad_query),
            rows_sum(grad_value),
        ],
        axis=0,
    )
    tail_all = lax.all_gather(tail_part.astype(BF), ("dp", "gy", "gx"), axis=0).astype(F32)
    grad_mod = jnp.sum(tail_all[:, :6].reshape(-1, span, 6, width), axis=1)
    grad_ada_b = jnp.sum(grad_mod, axis=0)
    tail_sum = jnp.sum(tail_all[:, 6:], axis=0)
    grad_query_b = lax.dynamic_slice_in_dim(tail_sum[0], at_gy * cols, cols, 0)
    grad_value_b = lax.dynamic_slice_in_dim(tail_sum[1], at_gy * cols, cols, 0)
    early_sum = lax.psum(
        jnp.concatenate([rows_sum(grad_mlp), rows_sum(grad_attn), rows_sum(grad_up_pre)], axis=0),
        ("gx", "gy", "dp"),
    )
    grad_down_b = lax.dynamic_slice_in_dim(early_sum[0], at_gx * width_x, width_x, 0)
    grad_out_b = lax.dynamic_slice_in_dim(early_sum[1], at_gx * width_x, width_x, 0)
    up_cols = up_bias.shape[0]
    grad_up_b = lax.dynamic_slice_in_dim(early_sum[2:].reshape(-1), at_gy * up_cols, up_cols, 0)

    mod_here = lax.dynamic_slice_in_dim(
        grad_mod, lax.axis_index("dp") * latent_count, latent_count, 0
    ).astype(BF)
    silu_every = lax.all_gather(silu_cond, "dp", axis=0, tiled=True)
    grad_ada_w = dot("le,lmf->emf", silu_every, grad_mod.astype(BF))
    grad_silu = dot("lmf,emf->le", mod_here, ada_weight)
    sigmoid_cond = jax.nn.sigmoid(cond_f32)
    grad_condition = grad_silu * sigmoid_cond * (1.0 + cond_f32 * (1.0 - sigmoid_cond))

    factor = TAU / jnp.maximum(logit_max, TAU)
    root_cols = jnp.repeat(jnp.sqrt(factor), HD)
    clipped_query = query_weight.astype(F32) * root_cols[None, :]
    clipped_key = key_weight.astype(F32) * root_cols[None, :]
    clipped_bias = query_bias * root_cols
    return (
        block_out,
        grad_input,
        grad_condition,
        grad_ada_w,
        grad_ada_b,
        grad_attn_w[:, :cols],
        grad_attn_w[:, cols : 2 * cols],
        grad_attn_w[:, 2 * cols : 3 * cols],
        grad_query_b,
        grad_value_b,
        grad_attn_w[:, 3 * cols :].T,
        grad_out_b,
        grad_up_w,
        grad_up_b,
        grad_down_w.T,
        grad_down_b,
        logit_max,
        clipped_query,
        clipped_key,
        clipped_bias,
    )


def solution(mesh):
    placed = (
        P(("dp", "gy", "gx"), None),
        P("dp", "gy"),
        P("gy", None, None),
        P(),
        P("gx", "gy"),
        P("gx", "gy"),
        P("gx", "gy"),
        P("gy"),
        P("gy"),
        P("gy", "gx"),
        P("gx"),
        P("gx", "gy"),
        P("gy"),
        P("gy", "gx"),
        P("gx"),
        P(("dp", "gy", "gx"), None),
    )
    return jax.shard_map(
        body,
        mesh=mesh,
        in_specs=placed,
        out_specs=(
            P(("dp", "gy", "gx"), None),
            P(("dp", "gy", "gx"), None),
            P("dp", "gy"),
            P("gy", None, None),
            P(),
            P("gx", "gy"),
            P("gx", "gy"),
            P("gx", "gy"),
            P("gy"),
            P("gy"),
            P("gy", "gx"),
            P("gx"),
            P("gx", "gy"),
            P("gy"),
            P("gy", "gx"),
            P("gx"),
            P("gy"),
            P("gx", "gy"),
            P("gx", "gy"),
            P("gy"),
        ),
        check_vma=False,
    )
```

```python
import math

import jax
import jax.numpy as jnp
from jax import lax
from jax.experimental import pallas as pl
from jax.experimental.pallas import tpu as pltpu
from jax.sharding import PartitionSpec as P

HD = 72
SEQ = 1024
TAU = 8

EPS = 1e-06
GELU_ROOT = 0.7978845608028654
GELU_CUBE = 0.044715
BF = jnp.bfloat16
F32 = jnp.float32
EVERY = ("gy", "gx", "dp")


def gelu_parts(inputs):
    inner_arg = GELU_ROOT * (inputs + GELU_CUBE * inputs * inputs * inputs)
    tangent = jnp.tanh(inner_arg)
    output = 0.5 * inputs * (1.0 + tangent)
    slope_rows = 0.5 * (1.0 + tangent) + 0.5 * inputs * (1.0 - tangent * tangent) * GELU_ROOT * (
        1.0 + 3.0 * GELU_CUBE * inputs * inputs
    )
    return (output, slope_rows)


def normalize(rows_in):
    mean_row = jnp.mean(rows_in, axis=1, keepdims=True)
    centred = rows_in - mean_row
    inverse = lax.rsqrt(jnp.mean(centred * centred, axis=1, keepdims=True) + EPS)
    return (centred * inverse, inverse)


def normalize_back(grad_hat, normed, inverse):
    grad_mean = jnp.mean(grad_hat, axis=1, keepdims=True)
    cross_mean = jnp.mean(grad_hat * normed, axis=1, keepdims=True)
    return inverse * (grad_hat - grad_mean - normed * cross_mean)


def swap(values, axis, bit):
    pairs = [(i, i ^ bit) for i in range(lax.axis_size(axis))]
    return lax.ppermute(values, axis, pairs)


def bits_of(axis):
    return [1 << k for k in range(lax.axis_size(axis).bit_length() - 1)]


def cube_gather(values, axis):
    at = lax.axis_index(axis)
    for bit in bits_of(axis):
        other = swap(values, axis, bit)
        low = (at & bit) == 0
        values = jnp.concatenate(
            [jnp.where(low, values, other), jnp.where(low, other, values)], axis=0
        )
    return values


def by_distance(values, index):
    count = values.shape[0]
    for k in range(count.bit_length() - 1):
        pairs = values.reshape((-1, 2, 1 << k) + values.shape[1:])
        flipped = jnp.concatenate([pairs[:, 1:], pairs[:, :1]], axis=1).reshape(values.shape)
        values = jnp.where((index >> k) & 1 == 1, flipped, values)
    return values


def total_steps(values):
    summed = lax.broadcasted_iota(jnp.int32, values.shape, 0) < values.shape[0] - 1
    for axis in ("dp", "gx", "gy"):
        for bit in bits_of(axis):
            values, got = yield (values, swap(values, axis, bit))
            values = jnp.where(summed, values + got, jnp.maximum(values, got))
    yield values


def pick(values, index, axis=0):
    return lax.dynamic_index_in_dim(values, index, axis, keepdims=False)


def add_low(left, right):
    return (left.astype(F32) + right.astype(F32)).astype(BF)


def own_half(shard):
    part = shard.shape[0] // 2
    return lax.dynamic_slice_in_dim(shard, lax.axis_index("dp") * part, part, 0)


def gather_weight(shard):
    full = lax.all_gather(own_half(shard), EVERY, axis=0, tiled=True)
    return full.reshape(lax.axis_size("gy"), -1, shard.shape[1])


def join_pair(values, other, axis, bit):
    low = (lax.axis_index(axis) & bit) == 0
    return jnp.stack([jnp.where(low, values, other), jnp.where(low, other, values)])


def gather_steps(shard):
    mine = own_half(shard)
    cols = shard.shape[1]
    if (lax.axis_size("gy"), lax.axis_size("gx")) != (4, 4):
        yield gather_weight(shard)
        return
    mine, got = yield (mine, swap(mine, "gx", 2))
    pair = join_pair(mine, got, "gx", 2)
    pair, got = yield (pair, swap(pair, "gx", 1))
    quad = join_pair(pair, got, "gx", 1)
    one, two = quad[:, 0], quad[:, 1]
    one, two, got_one, got_two = yield (one, two, swap(one, "gy", 2), swap(two, "gy", 1))
    one, two = join_pair(one, got_one, "gy", 2), join_pair(two, got_two, "gy", 1)
    one, two, got_one, got_two = yield (one, two, swap(one, "gy", 1), swap(two, "gy", 2))
    one, two = join_pair(one, got_one, "gy", 1), join_pair(two, got_two, "gy", 2)
    one, two, got_one, got_two = yield (one, two, swap(one, "dp", 1), swap(two, "dp", 1))
    low = lax.axis_index("dp") == 0

    def rows_of(values, got):
        return jnp.stack([jnp.where(low, values, got), jnp.where(low, got, values)], axis=3)

    one = jnp.swapaxes(rows_of(one, got_one), 0, 1)
    yield jnp.stack([one, rows_of(two, got_two)], axis=2).reshape(4, -1, cols)


def cube_mesh():
    return (lax.axis_size("gy"), lax.axis_size("gx"), lax.axis_size("dp")) == (4, 4, 2)


def scatter_steps(lefts, picks, rights):
    size_gx = lax.axis_size("gx")
    at_gy, at_gx, at_dp = lax.axis_index("gy"), lax.axis_index("gx"), lax.axis_index("dp")
    if cube_mesh():
        other = weight_grads_near(lefts, picks, rights, 1 - at_dp)
        (got,) = yield (swap(other, "dp", 1),)
        one, send_one, two, send_two = weight_grads_near(lefts, picks, rights, at_dp, got)
        one, two, got_one, got_two = yield (
            one,
            two,
            swap(send_one, "gy", 1),
            swap(send_two, "gy", 2),
        )
        one, two, got_one, got_two = yield (
            add_low(one[0], got_one[0]),
            add_low(two[0], got_two[0]),
            swap(add_low(one[1], got_one[1]), "gy", 2),
            swap(add_low(two[1], got_two[1]), "gy", 1),
        )
        at_z1, at_z0 = at_gx // 2, at_gx % 2
        acc = jnp.stack([add_low(one, got_one), add_low(two, got_two)])
        acc = acc.reshape(2, 2, -1, acc.shape[2])
        acc, got = yield (pick(acc, at_z0, 1), swap(pick(acc, 1 - at_z0, 1), "gx", 1))
        acc = add_low(acc, got)
        acc, got = yield (pick(acc, at_z1), swap(pick(acc, 1 - at_z1), "gx", 2))
        acc = add_low(acc, got)
    else:
        other, mine = [
            weight_grads([half_rows(x, w) for x in lefts], picks, rights)
            for w in (1 - at_dp, at_dp)
        ]
        got, mine = yield (swap(other, "dp", 1), mine)
        acc = add_low(mine, got)
        acc = lax.psum_scatter(
            acc.reshape(-1, acc.shape[2]), ("gy", "gx"), scatter_dimension=0, tiled=True
        )
    acc, got = yield (acc, swap(acc, "dp", 1))
    low = at_dp == 0
    yield jnp.concatenate([jnp.where(low, acc, got), jnp.where(low, got, acc)], axis=0).astype(F32)


class Exchange:
    def __init__(self, steps):
        self.steps = steps
        self.state = next(self.steps)
        self.done = not isinstance(self.state, tuple)

    def advance(self):
        self.state = self.steps.send(self.state)
        self.done = not isinstance(self.state, tuple)

    def result(self):
        while not self.done:
            self.advance()
        return self.state


def tick(value, *exchanges):
    live = [x for x in exchanges if not x.done]
    if not live:
        return value
    value, states = lax.optimization_barrier((value, [x.state for x in live]))
    for x, state in zip(live, states):
        x.state = state
        x.advance()
    return value


def half_rows(values, which):
    width, rows = values.shape
    blocks = values.reshape(lax.axis_size("gx"), 2, -1, rows)
    return pick(blocks, which, 1).reshape(width // 2, rows)


LOG2E = 1.4426950408889634
SCALE = 1.0 / math.sqrt(HD)


def dot(spec, left, right):
    return jnp.einsum(spec, left, right, preferred_element_type=F32)


def dot_t(left, right):
    return lax.dot_general(left, right, (((1,), (1,)), ((), ())), preferred_element_type=F32)


def dot_n(left, right):
    return jnp.dot(left, right, preferred_element_type=F32)


def by_group(kernel, name, whole, grouped, outs, flops, whole_out=None, scratch=()):
    g = grouped[0].shape[0]

    def block(x):
        return pl.BlockSpec((1,) + tuple(x.shape[1:]), lambda i: (i, 0, 0))

    shapes = [jax.ShapeDtypeStruct((g,) + shape, kind) for shape, kind in outs]
    specs = [block(x) for x in shapes]
    if whole_out is not None:
        shapes.append(jax.ShapeDtypeStruct(whole_out, F32))
        specs.append(pl.BlockSpec(whole_out, lambda i: (0, 0)))
    moved = sum(x.size * x.dtype.itemsize for x in [*whole, *grouped, *shapes])
    return pl.pallas_call(
        kernel,
        out_shape=shapes,
        grid=(g,),
        in_specs=[pl.BlockSpec(x.shape, lambda i: (0, 0)) for x in whole]
        + [block(x) for x in grouped],
        out_specs=specs,
        scratch_shapes=scratch,
        cost_estimate=pl.CostEstimate(flops=flops * g, transcendentals=0, bytes_accessed=moved),
        name=name,
    )(*whole, *grouped)


def edges_of(rights):
    edges = [0]
    for right in rights:
        edges.append(edges[-1] + right.shape[2])
    return edges


def weight_grads(lefts, picks, rights):
    m, edges = lefts[0].shape[0], edges_of(rights)

    def kernel(*refs):
        for i, k in enumerate(picks):
            right = refs[len(lefts) + i][0]
            refs[-1][0, :, edges[i] : edges[i + 1]] = dot_n(
                refs[k][:, : right.shape[0]], right
            ).astype(BF)

    flops = sum(2 * m * x.shape[1] * x.shape[2] for x in rights)
    return by_group(kernel, "weight_grads", lefts, rights, [((m, edges[-1]), BF)], flops)[0]


def weight_grads_near(lefts, picks, rights, side, got=None):
    size_gx = lax.axis_size("gx")
    lefts = [x.reshape(size_gx, 2, -1, x.shape[1]) for x in lefts]
    m, edges = size_gx * lefts[0].shape[2], edges_of(rights)
    n, part = edges[-1], m // 2

    def kernel(place_ref, *refs):
        left_refs, right_refs = refs[: len(lefts)], refs[len(lefts) : len(lefts) + len(rights)]
        rest = refs[len(lefts) + len(rights) :]
        step = pl.program_id(0)

        def product(i):
            right = right_refs[i][0]
            left = left_refs[picks[i]][:, 0, :, : right.shape[0]]
            return dot_n(left.reshape(m, right.shape[0]), right)

        if got is None:
            for i in range(len(rights)):
                rest[0][0, :, edges[i] : edges[i + 1]] = product(i).astype(BF)
            return
        got_ref, one_ref, send_one_ref, two_ref, send_two_ref = rest[:5]
        sum_ref = rest[5]
        for i in range(len(rights)):
            at = slice(edges[i], edges[i + 1])
            sum_ref[:, at] = (product(i) + got_ref[0, :, at].astype(F32)).astype(BF)

        for ref, rows, wanted in (
            (one_ref, slice(0, part), step % 2 == 0),
            (send_one_ref, slice(0, part), step % 2 == 1),
            (two_ref, slice(part, m), step // 2 == 0),
            (send_two_ref, slice(part, m), step // 2 == 1),
        ):

            @pl.when(wanted)
            def _(ref=ref, rows=rows):
                ref[0] = sum_ref[rows, :]

    place = jnp.stack([side, lax.axis_index("gy")]).astype(jnp.int32)
    in_specs = [
        pl.BlockSpec((size_gx, 1) + x.shape[2:], lambda i, p: (0, p[0], 0, 0)) for x in lefts
    ] + [pl.BlockSpec((1,) + x.shape[1:], lambda i, p: (i ^ p[1], 0, 0)) for x in rights]
    operands = [*lefts, *rights]
    scratch = []
    if got is None:
        shapes = jax.ShapeDtypeStruct((4, m, n), BF)
        out_specs = pl.BlockSpec((1, m, n), lambda i, p: (i, 0, 0))
    else:
        operands.append(got)
        in_specs.append(pl.BlockSpec((1, m, n), lambda i, p: (i, 0, 0)))
        shapes = [jax.ShapeDtypeStruct((2, part, n), BF)] * 4
        out_specs = [
            pl.BlockSpec((1, part, n), lambda i, p: (i // 2, 0, 0)),
            pl.BlockSpec((1, part, n), lambda i, p: (i // 2, 0, 0)),
            pl.BlockSpec((1, part, n), lambda i, p: (jnp.minimum(i, 1), 0, 0)),
            pl.BlockSpec((1, part, n), lambda i, p: (jnp.maximum(i, 2) - 2, 0, 0)),
        ]
        scratch = [pltpu.VMEM((m, n), BF)]
    flops = sum(8 * m * x.shape[1] * x.shape[2] for x in rights)
    moved = 8 * m * n * (1 if got is None else 2) + sum(2 * x.size for x in rights)
    return pl.pallas_call(
        kernel,
        out_shape=shapes,
        grid_spec=pltpu.PrefetchScalarGridSpec(
            num_scalar_prefetch=1,
            grid=(4,),
            in_specs=in_specs,
            out_specs=out_specs,
            scratch_shapes=scratch,
        ),
        cost_estimate=pl.CostEstimate(flops=flops, transcendentals=0, bytes_accessed=moved),
        name="weight_grads_near",
    )(place, *operands)


def project_back(xs, weight, terms, init=None):
    width, w_cols = weight.shape[1:]
    rows = xs[0].shape[1] if init is None else init.shape[0]
    rows = max([rows] + [x.shape[1] for x in xs])
    windows = []
    for x, start in zip(xs, terms):
        low = start // 128 * 128
        windows.append((low, min(-(-(start + x.shape[2]) // 128) * 128, w_cols), start - low))
    padded = [w[1] - w[0] != x.shape[2] for x, w in zip(xs, windows)]
    whole = [] if init is None else [init]

    def kernel(*refs):
        refs = list(refs)
        init_ref = refs.pop(0) if whole else None
        x_refs, w_ref, out_ref = refs[: len(xs)], refs[len(xs)], refs[len(xs) + 1]
        wide_refs = refs[len(xs) + 2 :]

        @pl.when(pl.program_id(0) == 0)
        def _():
            out_ref[...] = jnp.zeros((rows, width), F32) if init_ref is None else init_ref[...]
            for ref in wide_refs:
                ref[...] = jnp.zeros(ref.shape, BF)

        parts, wide = {}, 0
        for x_ref, (low, high, shift), pad in zip(x_refs, windows, padded):
            r, n = x_ref.shape[1:]
            if pad:
                ref = wide_refs[wide]
                wide += 1
                ref[:, shift : shift + n] = x_ref[0]
                x = ref[...]
            else:
                x = x_ref[0]
            part = dot_t(x, w_ref[0, :, low:high])
            parts[r] = parts[r] + part if r in parts else part
        for r, part in parts.items():
            out_ref[:r] += part

    scratch = [
        pltpu.VMEM((x.shape[1], w[1] - w[0]), BF) for x, w, pad in zip(xs, windows, padded) if pad
    ]
    flops = sum(2 * x.shape[1] * width * x.shape[2] for x in xs)
    return by_group(
        kernel, "project_back", whole, [*xs, weight], [], flops, (rows, width), scratch
    )[0]


def project_qkv(hidden, rows, weight, bias_q, bias_v):
    ctx, width = hidden.shape
    n = weight.shape[2] // 4

    def kernel(h_ref, w_ref, bq_ref, bv_ref, q_ref, k_ref, v_ref):
        joint = dot_n(h_ref[...], w_ref[0, :, : 3 * n])
        q_ref[0] = (joint[:rows, :n] + bq_ref[0]).astype(BF)
        k_ref[0] = joint[:, n : 2 * n].astype(BF)
        v_ref[0] = (joint[:, 2 * n :] + bv_ref[0]).astype(BF)

    return by_group(
        kernel,
        "project_qkv",
        [hidden],
        [weight, bias_q, bias_v],
        [((rows, n), BF), ((ctx, n), BF), ((ctx, n), BF)],
        6 * ctx * width * n,
    )


def project_up(hidden, weight, bias):
    rows, width = hidden.shape
    n = bias.shape[2]

    def kernel(h_ref, w_ref, bias_ref, act_ref, slope_ref):
        activ, slope = gelu_parts(dot_n(h_ref[...], w_ref[0]) + bias_ref[0])
        act_ref[0] = activ.astype(BF)
        slope_ref[0] = slope.astype(BF)

    return by_group(
        kernel,
        "project_up",
        [hidden],
        [weight, bias],
        [((rows, n), BF), ((rows, n), BF)],
        2 * rows * width * n,
    )


def project_act_back(grad_mlp, weight, slope):
    rows, width = grad_mlp.shape
    n = slope.shape[2]

    def kernel(g_ref, w_ref, slope_ref, low_ref, sums_ref):
        grad = dot_n(g_ref[...], w_ref[0]) * slope_ref[0].astype(F32)
        low_ref[0] = grad.astype(BF)
        sums_ref[0] = jnp.sum(grad, axis=0, keepdims=True)

    return by_group(
        kernel,
        "project_act_back",
        [grad_mlp],
        [weight, slope],
        [((rows, n), BF), ((1, n), F32)],
        2 * rows * width * n,
    )


def project_mixed_back(grad_attn, weight):
    rows, width = grad_attn.shape
    n = weight.shape[2] // 4
    low = 3 * n // 128 * 128

    def kernel(g_ref, w_ref, out_ref):
        out_ref[0] = dot_n(g_ref[...], w_ref[0, :, low:])[:, 3 * n - low :].astype(BF)

    return by_group(
        kernel, "project_mixed_back", [grad_attn], [weight], [((rows, n), BF)], 2 * rows * width * n
    )[0]


def head_of(ref, h):
    return ref[0, :, h * HD : (h + 1) * HD]


def attend(queries, keys_ctx, values_ctx):
    _, rows, n = queries.shape
    ctx = keys_ctx.shape[1]
    heads = n // HD

    def kernel(q_ref, k_ref, v_ref, mixed_ref, sums_ref, tops_ref):
        for h in range(heads):
            q, k, v = head_of(q_ref, h), head_of(k_ref, h), head_of(v_ref, h)
            scores = dot_t(k, q)
            top = jnp.max(scores, axis=0, keepdims=True)
            weights = jnp.exp2((scores - top) * (SCALE * LOG2E))
            total = jnp.sum(weights, axis=0, keepdims=True)
            mixed = dot_n(v.T, weights.astype(BF)) / total
            mixed_ref[0, :, h * HD : (h + 1) * HD] = mixed.T.astype(BF)
            sums_ref[0, h : h + 1, :] = top * (SCALE * LOG2E) + jnp.log2(total)
            tops_ref[0, h : h + 1, :] = top * SCALE

    return by_group(
        kernel,
        "attend",
        [],
        [queries, keys_ctx, values_ctx],
        [((rows, n), BF), ((heads, rows), F32), ((heads, rows), F32)],
        14 * rows * ctx * n,
    )


def attend_back(queries, keys_ctx, values_ctx, mixed, grad_mixed, log_sums, heads):
    _, rows, n = queries.shape
    ctx = keys_ctx.shape[1]
    n_out = len(heads) * HD

    def kernel(q_ref, k_ref, v_ref, x_ref, g_ref, sums_ref, gq_ref, gk_ref, gv_ref):
        for j, h in enumerate(heads):
            q, k, v = head_of(q_ref, h), head_of(k_ref, h), head_of(v_ref, h)
            grad = head_of(g_ref, h)
            delta = jnp.sum(
                (head_of(x_ref, h).astype(F32) * grad.astype(F32)).T, axis=0, keepdims=True
            )
            probs = jnp.exp2(dot_t(k, q) * (SCALE * LOG2E) - sums_ref[0, h : h + 1, :])
            grad_scores = (probs * (dot_t(v, grad) - delta)).astype(BF)
            out = slice(j * HD, (j + 1) * HD)
            gk_ref[0, :, out] = (dot_n(grad_scores, q) * SCALE).astype(BF)
            gv_ref[0, :, out] = dot_n(probs.astype(BF), grad).astype(BF)
            gq_ref[0, :, out] = (dot_n(k.T, grad_scores) * SCALE).T.astype(BF)

    return by_group(
        kernel,
        "attend_back",
        [],
        [queries, keys_ctx, values_ctx, mixed, grad_mixed, log_sums],
        [((rows, n_out), BF), ((ctx, n_out), BF), ((ctx, n_out), BF)],
        35 * rows * ctx * n_out,
    )


def body(
    latents_in,
    condition,
    ada_weight,
    ada_bias,
    query_weight,
    key_weight,
    value_weight,
    query_bias,
    value_bias,
    out_weight,
    out_bias,
    up_weight,
    up_bias,
    down_weight,
    down_bias,
    grad_out,
):
    rows, width = latents_in.shape
    latent_count = condition.shape[0]
    cols = query_weight.shape[1]
    width_x = out_bias.shape[0]
    size_gx, size_gy = lax.axis_size("gx"), lax.axis_size("gy")
    at_gx, at_gy = lax.axis_index("gx"), lax.axis_index("gy")
    span = SEQ // rows
    heads_here = cols // HD

    def rows_sum(values):
        return jnp.sum(values, axis=-2).reshape(-1, width)

    def shift_pairs(shift):
        return [(i, i // span * span + (i + shift) % span) for i in range(size_gx)]

    context = jnp.concatenate(
        [latents_in] + [lax.ppermute(latents_in, "gx", shift_pairs(s)) for s in range(1, span)], axis=0
    )

    cond_f32 = condition.astype(F32)
    silu_cond = jax.nn.silu(cond_f32).astype(BF)
    mod_part = dot("le,emf->lmf", silu_cond, ada_weight)
    for bit in reversed(bits_of("gy")):
        mod_pair = mod_part.reshape((2, -1) + mod_part.shape[1:])
        side = (at_gy // bit) % 2
        mod_part = pick(mod_pair, side) + swap(pick(mod_pair, 1 - side), "gy", bit)
    mod_own = pick(mod_part, at_gx // span) + ada_bias
    shift_one, scale_one, gate_one, shift_two, scale_two, gate_two = [
        mod_own[m : m + 1] for m in range(6)
    ]

    along_x = cube_gather(jnp.concatenate([out_bias, down_bias])[None], "gx")
    out_bias_all = along_x[:, :width_x].reshape(1, width)
    down_bias_all = along_x[:, width_x:].reshape(1, width)
    rest = cube_gather(jnp.concatenate([query_bias, value_bias, up_bias])[None], "gy")
    query_bias_all = rest[:, None, :cols]
    value_bias_all = rest[:, None, cols : 2 * cols]
    up_bias_all = rest[:, None, 2 * cols :]

    attn_w = gather_weight(
        jnp.concatenate([query_weight, key_weight, value_weight, out_weight.T], axis=1)
    )
    bring_up = Exchange(gather_steps(up_weight))
    down_w = gather_weight(down_weight.T)
    grad_mlp = gate_two * grad_out
    grad_mlp_low = grad_mlp.astype(BF)

    normed_ctx, inverse_ctx = normalize(context.astype(F32))
    hidden_ctx = (normed_ctx * (1.0 + scale_one) + shift_one).astype(BF)
    normed_one, inverse_one, hidden_one = normed_ctx[:rows], inverse_ctx[:rows], hidden_ctx[:rows]
    residual = latents_in.astype(F32)
    hidden_ctx, hidden_t, grad_mlp_t = lax.optimization_barrier(
        (hidden_ctx, hidden_ctx.T, grad_mlp_low.T)
    )
    for _ in range(3):
        hidden_ctx = tick(hidden_ctx, bring_up)
    queries, keys_ctx, values_ctx = project_qkv(
        hidden_ctx, rows, attn_w, query_bias_all, value_bias_all
    )
    queries = tick(queries, bring_up)
    mixed, log_sums, head_tops = attend(queries, keys_ctx, values_ctx)
    head_tops = jnp.max(head_tops, axis=2)
    mixed = tick(mixed, bring_up)
    attn_out = project_back([mixed], attn_w, [3 * cols]) + out_bias_all
    after_attn = residual + gate_one * attn_out
    normed_two, inverse_two = normalize(after_attn)
    hidden_two = (normed_two * (1.0 + scale_two) + shift_two).astype(BF)
    up_w = bring_up.result()
    activation, gelu_slope = project_up(hidden_two, up_w, up_bias_all)
    sum_down = Exchange(scatter_steps([grad_mlp_t], [0], [activation]))
    grad_up_low, up_sums = project_act_back(grad_mlp_low, down_w, gelu_slope)
    grad_up_low = tick(grad_up_low, sum_down)
    sum_up = Exchange(scatter_steps([hidden_two.T], [0], [grad_up_low]))
    grad_hidden_two = project_back([grad_up_low], up_w, [0])
    grad_hidden_two = tick(grad_hidden_two, sum_down, sum_up)
    grad_after = grad_out + normalize_back(
        grad_hidden_two * (1.0 + scale_two), normed_two, inverse_two
    )
    grad_attn = gate_one * grad_after
    grad_attn_low = grad_attn.astype(BF)
    grad_mixed_low = project_mixed_back(grad_attn_low, attn_w)
    grad_attn_t = grad_attn_low.T
    tops_row = jnp.zeros((1, width), F32).at[0, : size_gy * heads_here].set(head_tops.reshape(-1))
    early = Exchange(
        total_steps(
            jnp.concatenate(
                [rows_sum(grad_mlp), rows_sum(grad_attn), up_sums.reshape(-1, width), tops_row],
                axis=0,
            )
        )
    )

    half = (heads_here + 1) // 2
    head_sets = [x for x in (range(half), range(half, heads_here)) if len(x)]
    sum_attn, back_parts, grad_ctx = [], [], None
    for i, heads in enumerate(head_sets):
        parts = attend_back(queries, keys_ctx, values_ctx, mixed, grad_mixed_low, log_sums, heads)
        parts = tick(parts, early, sum_down, sum_up, *sum_attn)
        back_parts.append(parts)
        extra = i == 0
        sum_attn.append(
            Exchange(
                scatter_steps(
                    [hidden_t] + [grad_attn_t] * extra,
                    [0, 0, 0] + [1] * extra,
                    list(parts) + [mixed] * extra,
                )
            )
        )
        start = heads[0] * HD
        grad_ctx = project_back(
            list(parts), attn_w, [start, cols + start, 2 * cols + start], grad_ctx
        )
        if i + 1 < len(head_sets):
            grad_mixed_low, grad_ctx = tick(
                (grad_mixed_low, grad_ctx), early, sum_down, sum_up, *sum_attn
            )
    grad_ctx, activation = tick((grad_ctx, activation), early, sum_down, sum_up, *sum_attn)
    grad_hidden_one = grad_ctx[:rows]
    for s in range(1, span):
        back = [(b, a) for a, b in shift_pairs(s)]
        grad_hidden_one += lax.ppermute(
            grad_ctx[s * rows : (s + 1) * rows].astype(BF), "gx", back
        ).astype(F32)
    mlp_out = project_back([activation], down_w, [0]) + down_bias_all
    mlp_out, grad_hidden_one = tick((mlp_out, grad_hidden_one), early, sum_up, *sum_attn)
    block_out = after_attn + gate_two * mlp_out
    grad_input = grad_after + normalize_back(
        grad_hidden_one * (1.0 + scale_one), normed_one, inverse_one
    )

    def group_sum(i):
        return jnp.concatenate(
            [jnp.sum(x[i].astype(F32), axis=1) for x in back_parts], axis=1
        ).reshape(1, width)

    late = jnp.concatenate(
        [
            rows_sum(grad_hidden_one),
            rows_sum(grad_hidden_one * normed_one),
            rows_sum(grad_after * attn_out),
            rows_sum(grad_hidden_two),
            rows_sum(grad_hidden_two * normed_two),
            rows_sum(grad_out * mlp_out),
            group_sum(0),
            group_sum(2),
        ],
        axis=0,
    )
    for bit in bits_of("gx"):
        if bit < span:
            late = late + swap(late, "gx", bit)
    late = late.astype(BF)[None]
    for axis in ("gx", "gy"):
        for bit in bits_of(axis):
            if axis == "gy" or bit >= span:
                late = jnp.concatenate([late, swap(late, axis, bit)], axis=0)
    late_all = jnp.concatenate([late, swap(late, "dp", 1)], axis=0)
    at_latent = at_gy * (size_gx // span) + at_gx // span
    grad_ada_b = jnp.sum(late_all[:, :6].astype(F32), axis=0)
    tail_sum = jnp.sum(late_all[:, 6:].astype(F32), axis=0)
    grad_query_b = lax.dynamic_slice_in_dim(tail_sum[0], at_gy * cols, cols, 0)
    grad_value_b = lax.dynamic_slice_in_dim(tail_sum[1], at_gy * cols, cols, 0)
    silu_near = by_distance(silu_cond, at_latent)
    silu_every = jnp.concatenate(
        [silu_near, by_distance(swap(silu_cond, "dp", 1), at_latent)], axis=0
    )
    grad_ada_w = dot("le,lmf->emf", silu_every, late_all[:, :6])
    grad_silu = by_distance(dot("lmf,emf->le", late[:, :6], ada_weight), at_latent)
    sigmoid_cond = jax.nn.sigmoid(cond_f32)
    grad_condition = grad_silu * sigmoid_cond * (1.0 + cond_f32 * (1.0 - sigmoid_cond))

    early_sum = early.result()
    grad_down_b = lax.dynamic_slice_in_dim(early_sum[0], at_gx * width_x, width_x, 0)
    grad_out_b = lax.dynamic_slice_in_dim(early_sum[1], at_gx * width_x, width_x, 0)
    up_cols = up_bias.shape[0]
    grad_up_b = lax.dynamic_slice_in_dim(early_sum[2:-1].reshape(-1), at_gy * up_cols, up_cols, 0)
    logit_max = lax.dynamic_slice_in_dim(early_sum[-1], at_gy * heads_here, heads_here, 0)

    grad_down_w, grad_up_w = sum_down.result(), sum_up.result()
    sums = [x.result() for x in sum_attn]
    grad_qkv = [
        jnp.concatenate(
            [x[:, i * HD * len(h) : (i + 1) * HD * len(h)] for x, h in zip(sums, head_sets)], axis=1
        )
        for i in range(3)
    ]
    grad_out_w = sums[0][:, 3 * HD * len(head_sets[0]) :]

    factor = TAU / jnp.maximum(logit_max, TAU)
    root_cols = jnp.repeat(jnp.sqrt(factor), HD)
    clipped_query = query_weight.astype(F32) * root_cols[None, :]
    clipped_key = key_weight.astype(F32) * root_cols[None, :]
    clipped_bias = query_bias * root_cols
    return (
        block_out,
        grad_input,
        grad_condition,
        grad_ada_w,
        grad_ada_b,
        *grad_qkv,
        grad_query_b,
        grad_value_b,
        grad_out_w.T,
        grad_out_b,
        grad_up_w,
        grad_up_b,
        grad_down_w.T,
        grad_down_b,
        logit_max,
        clipped_query,
        clipped_key,
        clipped_bias,
    )


def solution(mesh):
    placed = (
        P(("dp", "gy", "gx"), None),
        P("dp", "gy"),
        P("gy", None, None),
        P(),
        P("gx", "gy"),
        P("gx", "gy"),
        P("gx", "gy"),
        P("gy"),
        P("gy"),
        P("gy", "gx"),
        P("gx"),
        P("gx", "gy"),
        P("gy"),
        P("gy", "gx"),
        P("gx"),
        P(("dp", "gy", "gx"), None),
    )
    return jax.shard_map(
        body,
        mesh=mesh,
        in_specs=placed,
        out_specs=(
            P(("dp", "gy", "gx"), None),
            P(("dp", "gy", "gx"), None),
            P("dp", "gy"),
            P("gy", None, None),
            P(),
            P("gx", "gy"),
            P("gx", "gy"),
            P("gx", "gy"),
            P("gy"),
            P("gy"),
            P("gy", "gx"),
            P("gx"),
            P("gx", "gy"),
            P("gy"),
            P("gy", "gx"),
            P("gx"),
            P("gy"),
            P("gx", "gy"),
            P("gx", "gy"),
            P("gy"),
        ),
        check_vma=False,
    )
```

```python
import math

import jax
import jax.numpy as jnp
from jax import lax
from jax.experimental import pallas as pl
from jax.experimental.pallas import tpu as pltpu
from jax.sharding import PartitionSpec as P

HD = 72
SEQ = 1024
TAU = 8

EPS = 1e-06
GELU_ROOT = 0.7978845608028654
GELU_CUBE = 0.044715
BF = jnp.bfloat16
F32 = jnp.float32
EVERY = ("gy", "gx", "dp")


def gelu_parts(inputs):
    inner_arg = GELU_ROOT * (inputs + GELU_CUBE * inputs * inputs * inputs)
    tangent = jnp.tanh(inner_arg)
    output = 0.5 * inputs * (1.0 + tangent)
    slope_rows = 0.5 * (1.0 + tangent) + 0.5 * inputs * (1.0 - tangent * tangent) * GELU_ROOT * (
        1.0 + 3.0 * GELU_CUBE * inputs * inputs
    )
    return (output, slope_rows)


def normalize(rows_in):
    mean_row = jnp.mean(rows_in, axis=1, keepdims=True)
    centred = rows_in - mean_row
    inverse = lax.rsqrt(jnp.mean(centred * centred, axis=1, keepdims=True) + EPS)
    return (centred * inverse, inverse)


def normalize_back(grad_hat, normed, inverse):
    grad_mean = jnp.mean(grad_hat, axis=1, keepdims=True)
    cross_mean = jnp.mean(grad_hat * normed, axis=1, keepdims=True)
    return inverse * (grad_hat - grad_mean - normed * cross_mean)


def swap(values, axis, bit):
    pairs = [(i, i ^ bit) for i in range(lax.axis_size(axis))]
    return lax.ppermute(values, axis, pairs)


def bits_of(axis):
    return [1 << k for k in range(lax.axis_size(axis).bit_length() - 1)]


def cube_gather(values, axis):
    at = lax.axis_index(axis)
    for bit in bits_of(axis):
        other = swap(values, axis, bit)
        low = (at & bit) == 0
        values = jnp.concatenate(
            [jnp.where(low, values, other), jnp.where(low, other, values)], axis=0
        )
    return values


def by_distance(values, index):
    count = values.shape[0]
    for k in range(count.bit_length() - 1):
        pairs = values.reshape((-1, 2, 1 << k) + values.shape[1:])
        flipped = jnp.concatenate([pairs[:, 1:], pairs[:, :1]], axis=1).reshape(values.shape)
        values = jnp.where((index >> k) & 1 == 1, flipped, values)
    return values


def total_steps(values):
    summed = lax.broadcasted_iota(jnp.int32, values.shape, 0) < values.shape[0] - 1
    for axis in ("dp", "gx", "gy"):
        for bit in bits_of(axis):
            values, got = yield (values, swap(values, axis, bit))
            values = jnp.where(summed, values + got, jnp.maximum(values, got))
    yield values


def pick(values, index, axis=0):
    return lax.dynamic_index_in_dim(values, index, axis, keepdims=False)


def add_low(left, right):
    return (left.astype(F32) + right.astype(F32)).astype(BF)


def own_half(shard):
    part = shard.shape[0] // 2
    return lax.dynamic_slice_in_dim(shard, lax.axis_index("dp") * part, part, 0)


def gather_weight(shard):
    full = lax.all_gather(own_half(shard), EVERY, axis=0, tiled=True)
    return full.reshape(lax.axis_size("gy"), -1, shard.shape[1])


def cube_mesh():
    return (lax.axis_size("gy"), lax.axis_size("gx"), lax.axis_size("dp")) == (4, 4, 2)


def scatter_steps(order, lefts, picks, rights):
    size_gx = lax.axis_size("gx")
    at_gy, at_gx, at_dp = lax.axis_index("gy"), lax.axis_index("gx"), lax.axis_index("dp")
    if cube_mesh():
        other = weight_grads_near(order, lefts, picks, rights, 1 - at_dp)
        (got,) = yield (swap(other, "dp", 1),)
        one, send_one, two, send_two = weight_grads_near(order, lefts, picks, rights, at_dp, got)
        one, two, got_one, got_two = yield (
            one,
            two,
            swap(send_one, "gy", 1),
            swap(send_two, "gy", 2),
        )
        one, two, got_one, got_two = yield (
            add_low(one[0], got_one[0]),
            add_low(two[0], got_two[0]),
            swap(add_low(one[1], got_one[1]), "gy", 2),
            swap(add_low(two[1], got_two[1]), "gy", 1),
        )
        at_z1, at_z0 = at_gx // 2, at_gx % 2
        acc = jnp.stack([add_low(one, got_one), add_low(two, got_two)])
        acc = acc.reshape(2, 2, -1, acc.shape[2])
        acc, got = yield (pick(acc, at_z0, 1), swap(pick(acc, 1 - at_z0, 1), "gx", 1))
        acc = add_low(acc, got)
        acc, got = yield (pick(acc, at_z1), swap(pick(acc, 1 - at_z1), "gx", 2))
        acc = add_low(acc, got)
    else:
        other, mine = [
            weight_grads(order, [half_rows(x, w) for x in lefts], picks, rights)
            for w in (1 - at_dp, at_dp)
        ]
        got, mine = yield (swap(other, "dp", 1), mine)
        acc = add_low(mine, got)
        acc = lax.psum_scatter(
            acc.reshape(-1, acc.shape[2]), ("gy", "gx"), scatter_dimension=0, tiled=True
        )
    acc, got = yield (acc, swap(acc, "dp", 1))
    low = at_dp == 0
    yield jnp.concatenate([jnp.where(low, acc, got), jnp.where(low, got, acc)], axis=0).astype(F32)


class Exchange:
    def __init__(self, steps):
        self.steps = steps
        self.state = next(self.steps)
        self.done = not isinstance(self.state, tuple)

    def advance(self):
        self.state = self.steps.send(self.state)
        self.done = not isinstance(self.state, tuple)

    def result(self):
        while not self.done:
            self.advance()
        return self.state


class Order:
    def __init__(self):
        self.token = jnp.zeros((8, 128), F32)

    def tick(self, *exchanges):
        live = [x for x in exchanges if not x.done]
        self.token, states = lax.optimization_barrier((self.token, [x.state for x in live]))
        for x, state in zip(live, states):
            x.state = state
            x.advance()


ORDER_SPEC = pl.BlockSpec((8, 128), lambda *_: (0, 0))
ORDER_SHAPE = jax.ShapeDtypeStruct((8, 128), F32)


def half_rows(values, which):
    width, rows = values.shape
    blocks = values.reshape(lax.axis_size("gx"), 2, -1, rows)
    return pick(blocks, which, 1).reshape(width // 2, rows)


LOG2E = 1.4426950408889634
SCALE = 1.0 / math.sqrt(HD)


def dot(spec, left, right):
    return jnp.einsum(spec, left, right, preferred_element_type=F32)


def dot_t(left, right):
    return lax.dot_general(left, right, (((1,), (1,)), ((), ())), preferred_element_type=F32)


def dot_n(left, right):
    return jnp.dot(left, right, preferred_element_type=F32)


def by_group(order, kernel, name, whole, grouped, outs, flops, whole_outs=(), scratch=()):
    parts = [x[1] if isinstance(x, tuple) else (x.shape[2], 0) for x in grouped]
    grouped = [x[0] if isinstance(x, tuple) else x for x in grouped]
    g = grouped[0].shape[0]

    def block(rows, cols, k=0):
        return pl.BlockSpec((1, rows, cols), lambda i: (i, 0, k))

    def in_order(order_ref, *refs):
        inputs = len(whole) + len(grouped)
        refs[inputs][...] = order_ref[...]
        kernel(*refs[:inputs], *refs[inputs + 1 :])

    shapes = [jax.ShapeDtypeStruct((g,) + shape, kind) for shape, kind in outs]
    specs = [block(*x.shape[1:]) for x in shapes]
    for shape, kind in whole_outs:
        shapes.append(jax.ShapeDtypeStruct(shape, kind))
        specs.append(pl.BlockSpec(shape, lambda i: (0, 0)))
    moved = sum(x.size * x.dtype.itemsize for x in [*whole, *grouped, *shapes])
    order.token, *results = pl.pallas_call(
        in_order,
        out_shape=[ORDER_SHAPE, *shapes],
        grid=(g,),
        in_specs=[ORDER_SPEC]
        + [pl.BlockSpec(x.shape, lambda i: (0, 0)) for x in whole]
        + [block(x.shape[1], *part) for x, part in zip(grouped, parts)],
        out_specs=[ORDER_SPEC, *specs],
        scratch_shapes=scratch,
        cost_estimate=pl.CostEstimate(flops=flops * g, transcendentals=0, bytes_accessed=moved),
        name=name,
    )(order.token, *whole, *grouped)
    return results


def transposed(order, *arrays):
    count = len(arrays)

    def kernel(order_ref, *refs):
        refs[count][...] = order_ref[...]
        for x_ref, out_ref in zip(refs[:count], refs[count + 1 :]):
            out_ref[...] = x_ref[...].T

    order.token, *results = pl.pallas_call(
        kernel,
        out_shape=[ORDER_SHAPE, *[jax.ShapeDtypeStruct(x.shape[::-1], BF) for x in arrays]],
        name="transposed",
    )(order.token, *arrays)
    return results


def edges_of(rights):
    edges = [0]
    for right in rights:
        edges.append(edges[-1] + right.shape[2])
    return edges


def weight_grads(order, lefts, picks, rights):
    m, edges = lefts[0].shape[0], edges_of(rights)

    def kernel(*refs):
        for i, k in enumerate(picks):
            right = refs[len(lefts) + i][0]
            refs[-1][0, :, edges[i] : edges[i + 1]] = dot_n(
                refs[k][:, : right.shape[0]], right
            ).astype(BF)

    flops = sum(2 * m * x.shape[1] * x.shape[2] for x in rights)
    return by_group(order, kernel, "weight_grads", lefts, rights, [((m, edges[-1]), BF)], flops)[0]


def weight_grads_near(order, lefts, picks, rights, side, got=None):
    size_gx = lax.axis_size("gx")
    lefts = [x.reshape(size_gx, 2, -1, x.shape[1]) for x in lefts]
    m, edges = size_gx * lefts[0].shape[2], edges_of(rights)
    n, part = -(-edges[-1] // 128) * 128, m // 2

    def kernel(place_ref, order_ref, *refs):
        left_refs, right_refs = refs[: len(lefts)], refs[len(lefts) : len(lefts) + len(rights)]
        rest = refs[len(lefts) + len(rights) :]
        if got is not None:
            got_ref, rest = rest[0], rest[1:]
        step = pl.program_id(0)
        rest[0][...] = order_ref[...]
        rest = rest[1:]

        def product(i):
            right = right_refs[i][0]
            left = left_refs[picks[i]][:, 0, :, : right.shape[0]]
            return dot_n(left.reshape(m, right.shape[0]), right)

        if got is None:
            for i in range(len(rights)):
                rest[0][0, :, edges[i] : edges[i + 1]] = product(i).astype(BF)
            if n > edges[-1]:
                rest[0][0, :, edges[-1] :] = jnp.zeros((m, n - edges[-1]), BF)
            return
        one_ref, send_one_ref, two_ref, send_two_ref, sum_ref = rest
        for i in range(len(rights)):
            at = slice(edges[i], edges[i + 1])
            sum_ref[:, at] = (product(i) + got_ref[0, :, at].astype(F32)).astype(BF)
        if n > edges[-1]:
            sum_ref[:, edges[-1] :] = jnp.zeros((m, n - edges[-1]), BF)

        for ref, rows, wanted in (
            (one_ref, slice(0, part), step % 2 == 0),
            (send_one_ref, slice(0, part), step % 2 == 1),
            (two_ref, slice(part, m), step // 2 == 0),
            (send_two_ref, slice(part, m), step // 2 == 1),
        ):

            @pl.when(wanted)
            def _(ref=ref, rows=rows):
                ref[0] = sum_ref[rows, :]

    place = jnp.stack([side, lax.axis_index("gy")]).astype(jnp.int32)
    in_specs = [ORDER_SPEC] + [
        pl.BlockSpec((size_gx, 1) + x.shape[2:], lambda i, p: (0, p[0], 0, 0)) for x in lefts
    ] + [pl.BlockSpec((1,) + x.shape[1:], lambda i, p: (i ^ p[1], 0, 0)) for x in rights]
    operands = [order.token, *lefts, *rights]
    scratch = []
    if got is None:
        shapes = [jax.ShapeDtypeStruct((4, m, n), BF)]
        out_specs = [pl.BlockSpec((1, m, n), lambda i, p: (i, 0, 0))]
    else:
        operands.append(got)
        in_specs.append(pl.BlockSpec((1, m, n), lambda i, p: (i, 0, 0)))
        shapes = [jax.ShapeDtypeStruct((2, part, n), BF)] * 4
        out_specs = [
            pl.BlockSpec((1, part, n), lambda i, p: (i // 2, 0, 0)),
            pl.BlockSpec((1, part, n), lambda i, p: (i // 2, 0, 0)),
            pl.BlockSpec((1, part, n), lambda i, p: (jnp.minimum(i, 1), 0, 0)),
            pl.BlockSpec((1, part, n), lambda i, p: (jnp.maximum(i, 2) - 2, 0, 0)),
        ]
        scratch = [pltpu.VMEM((m, n), BF)]
    flops = sum(8 * m * x.shape[1] * x.shape[2] for x in rights)
    moved = 8 * m * n * (1 if got is None else 2) + sum(2 * x.size for x in rights)
    order.token, *results = pl.pallas_call(
        kernel,
        out_shape=[ORDER_SHAPE, *shapes],
        grid_spec=pltpu.PrefetchScalarGridSpec(
            num_scalar_prefetch=1,
            grid=(4,),
            in_specs=in_specs,
            out_specs=[ORDER_SPEC, *out_specs],
            scratch_shapes=scratch,
        ),
        cost_estimate=pl.CostEstimate(flops=flops, transcendentals=0, bytes_accessed=moved),
        name="weight_grads_near",
    )(place, *operands)
    return results[0] if got is None else results


def project_back(order, xs, weight, terms, init=None, own=None):
    weight, (w_cols, part) = weight if isinstance(weight, tuple) else (weight, (weight.shape[2], 0))
    width = weight.shape[1]
    rows = xs[0].shape[1] if init is None else init.shape[0]
    rows = max([rows] + [x.shape[1] for x in xs])
    windows = []
    for x, start in zip(xs, terms):
        low = start // 128 * 128
        windows.append((low, min(-(-(start + x.shape[2]) // 128) * 128, w_cols), start - low))
    padded = [w[1] - w[0] != x.shape[2] for x, w in zip(xs, windows)]
    whole = [] if init is None else [init]

    def kernel(*refs):
        refs = list(refs)
        init_ref = refs.pop(0) if whole else None
        x_refs, w_ref = refs[: len(xs)], refs[len(xs)]
        refs = refs[len(xs) + 1 :]
        low_ref = refs.pop(0) if own is not None else None
        out_ref, wide_refs = refs[0], refs[1:]

        @pl.when(pl.program_id(0) == 0)
        def _():
            out_ref[...] = jnp.zeros((rows, width), F32) if init_ref is None else init_ref[...]
            for ref in wide_refs:
                ref[...] = jnp.zeros(ref.shape, BF)

        parts, wide = {}, 0
        for x_ref, (low, high, shift), pad in zip(x_refs, windows, padded):
            r, n = x_ref.shape[1:]
            if pad:
                ref = wide_refs[wide]
                wide += 1
                ref[:, shift : shift + n] = x_ref[0]
                x = ref[...]
            else:
                x = x_ref[0]
            part = dot_t(x, w_ref[0, :, low:high])
            parts[r] = parts[r] + part if r in parts else part
        for r, part in parts.items():
            out_ref[:r] += part
        if low_ref is not None:

            @pl.when(pl.program_id(0) == pl.num_programs(0) - 1)
            def _():
                low_ref[...] = out_ref[own:].astype(BF)

    scratch = [
        pltpu.VMEM((x.shape[1], w[1] - w[0]), BF) for x, w, pad in zip(xs, windows, padded) if pad
    ]
    flops = sum(2 * x.shape[1] * width * x.shape[2] for x in xs)
    wholes = [] if own is None else [((rows - own, width), BF)]
    wholes.append(((rows, width), F32))
    results = by_group(
        order,
        kernel,
        "project_back",
        whole,
        [*xs, (weight, (w_cols, part))],
        [],
        flops,
        wholes,
        scratch,
    )
    return results[0] if own is None else results


def project_qkv(order, hidden, rows, weight, bias_q, bias_v):
    ctx, width = hidden.shape
    n = bias_q.shape[2]

    def kernel(h_ref, w_ref, bq_ref, bv_ref, q_ref, k_ref, v_ref):
        joint = dot_n(h_ref[...], w_ref[0, :, : 3 * n])
        q_ref[0] = (joint[:rows, :n] + bq_ref[0]).astype(BF)
        k_ref[0] = joint[:, n : 2 * n].astype(BF)
        v_ref[0] = (joint[:, 2 * n :] + bv_ref[0]).astype(BF)

    return by_group(
        order,
        kernel,
        "project_qkv",
        [hidden],
        [weight, bias_q, bias_v],
        [((rows, n), BF), ((ctx, n), BF), ((ctx, n), BF)],
        6 * ctx * width * n,
    )


def project_up(order, hidden, weight, bias):
    rows, width = hidden.shape
    n = bias.shape[2]

    def kernel(h_ref, w_ref, bias_ref, act_ref, slope_ref):
        activ, slope = gelu_parts(dot_n(h_ref[...], w_ref[0]) + bias_ref[0])
        act_ref[0] = activ.astype(BF)
        slope_ref[0] = slope.astype(BF)

    return by_group(
        order,
        kernel,
        "project_up",
        [hidden],
        [weight, bias],
        [((rows, n), BF), ((rows, n), BF)],
        2 * rows * width * n,
    )


def project_act_back(order, grad_mlp, weight, slope):
    rows, width = grad_mlp.shape
    n = slope.shape[2]

    def kernel(g_ref, w_ref, slope_ref, low_ref, sums_ref):
        grad = dot_n(g_ref[...], w_ref[0]) * slope_ref[0].astype(F32)
        low_ref[0] = grad.astype(BF)
        sums_ref[0] = jnp.sum(grad, axis=0, keepdims=True)

    return by_group(
        order,
        kernel,
        "project_act_back",
        [grad_mlp],
        [weight, slope],
        [((rows, n), BF), ((1, n), F32)],
        2 * rows * width * n,
    )


def project_mixed_back(order, grad_attn, weight, n, skip):
    rows, width = grad_attn.shape

    def kernel(g_ref, w_ref, out_ref):
        out_ref[0] = dot_n(g_ref[...], w_ref[0])[:, skip:].astype(BF)

    return by_group(
        order,
        kernel,
        "project_mixed_back",
        [grad_attn],
        [weight],
        [((rows, n), BF)],
        2 * rows * width * n,
    )[0]


def head_of(ref, h):
    return ref[0, :, h * HD : (h + 1) * HD]


def attend(order, queries, keys_ctx, values_ctx):
    _, rows, n = queries.shape
    ctx = keys_ctx.shape[1]
    heads = n // HD

    def kernel(q_ref, k_ref, v_ref, mixed_ref, sums_ref, tops_ref):
        for h in range(heads):
            q, k, v = head_of(q_ref, h), head_of(k_ref, h), head_of(v_ref, h)
            scores = dot_t(k, q)
            top = jnp.max(scores, axis=0, keepdims=True)
            weights = jnp.exp2((scores - top) * (SCALE * LOG2E))
            total = jnp.sum(weights, axis=0, keepdims=True)
            mixed = dot_n(v.T, weights.astype(BF)) / total
            mixed_ref[0, :, h * HD : (h + 1) * HD] = mixed.T.astype(BF)
            sums_ref[0, h : h + 1, :] = top * (SCALE * LOG2E) + jnp.log2(total)
            tops_ref[0, h : h + 1, :] = top * SCALE

    return by_group(
        order,
        kernel,
        "attend",
        [],
        [queries, keys_ctx, values_ctx],
        [((rows, n), BF), ((heads, rows), F32), ((heads, rows), F32)],
        14 * rows * ctx * n,
    )


def attend_back(order, queries, keys_ctx, values_ctx, mixed, grad_mixed, log_sums, heads):
    _, rows, n = queries.shape
    ctx = keys_ctx.shape[1]
    n_out = len(heads) * HD

    def kernel(q_ref, k_ref, v_ref, x_ref, g_ref, sums_ref, gq_ref, gk_ref, gv_ref):
        for j, h in enumerate(heads):
            q, k, v = head_of(q_ref, h), head_of(k_ref, h), head_of(v_ref, h)
            grad = head_of(g_ref, h)
            delta = jnp.sum(
                (head_of(x_ref, h).astype(F32) * grad.astype(F32)).T, axis=0, keepdims=True
            )
            probs = jnp.exp2(dot_t(k, q) * (SCALE * LOG2E) - sums_ref[0, h : h + 1, :])
            grad_scores = (probs * (dot_t(v, grad) - delta)).astype(BF)
            out = slice(j * HD, (j + 1) * HD)
            gk_ref[0, :, out] = (dot_n(grad_scores, q) * SCALE).astype(BF)
            gv_ref[0, :, out] = dot_n(probs.astype(BF), grad).astype(BF)
            gq_ref[0, :, out] = (dot_n(k.T, grad_scores) * SCALE).T.astype(BF)

    return by_group(
        order,
        kernel,
        "attend_back",
        [],
        [queries, keys_ctx, values_ctx, mixed, grad_mixed, log_sums],
        [((rows, n_out), BF), ((ctx, n_out), BF), ((ctx, n_out), BF)],
        35 * rows * ctx * n_out,
    )


def body(
    latents_in,
    condition,
    ada_weight,
    ada_bias,
    query_weight,
    key_weight,
    value_weight,
    query_bias,
    value_bias,
    out_weight,
    out_bias,
    up_weight,
    up_bias,
    down_weight,
    down_bias,
    grad_out,
):
    rows, width = latents_in.shape
    latent_count = condition.shape[0]
    cols = query_weight.shape[1]
    width_x = out_bias.shape[0]
    size_gx, size_gy = lax.axis_size("gx"), lax.axis_size("gy")
    at_gx, at_gy = lax.axis_index("gx"), lax.axis_index("gy")
    span = SEQ // rows
    heads_here = cols // HD

    def rows_sum(values):
        return jnp.sum(values, axis=-2).reshape(-1, width)

    def shift_pairs(shift):
        return [(i, i // span * span + (i + shift) % span) for i in range(size_gx)]

    context = jnp.concatenate(
        [latents_in] + [lax.ppermute(latents_in, "gx", shift_pairs(s)) for s in range(1, span)], axis=0
    )

    cond_f32 = condition.astype(F32)
    silu_cond = jax.nn.silu(cond_f32).astype(BF)
    mod_part = dot("le,emf->lmf", silu_cond, ada_weight)
    for bit in reversed(bits_of("gy")):
        mod_pair = mod_part.reshape((2, -1) + mod_part.shape[1:])
        side = (at_gy // bit) % 2
        mod_part = pick(mod_pair, side) + swap(pick(mod_pair, 1 - side), "gy", bit)
    mod_own = pick(mod_part, at_gx // span) + ada_bias
    shift_one, scale_one, gate_one, shift_two, scale_two, gate_two = [
        mod_own[m : m + 1] for m in range(6)
    ]

    along_x = cube_gather(jnp.concatenate([out_bias, down_bias])[None], "gx")
    out_bias_all = along_x[:, :width_x].reshape(1, width)
    down_bias_all = along_x[:, width_x:].reshape(1, width)
    rest = cube_gather(jnp.concatenate([query_bias, value_bias, up_bias])[None], "gy")
    query_bias_all = rest[:, None, :cols]
    value_bias_all = rest[:, None, cols : 2 * cols]
    up_bias_all = rest[:, None, 2 * cols :]

    order = Order()
    up_cols = up_bias.shape[0]
    attn_part = jnp.concatenate([query_weight, key_weight, value_weight, out_weight.T], axis=1)
    if up_cols == 4 * cols and up_cols % 128 == 0:
        joint_w = gather_weight(jnp.concatenate([attn_part, up_weight], axis=1))
        attn_w, up_w = (joint_w, (up_cols, 0)), (joint_w, (up_cols, 1))
    else:
        attn_w = (gather_weight(attn_part), (4 * cols, 0))
        up_w = (gather_weight(up_weight), (up_cols, 0))
    out_start = 3 * cols // 128 * 128
    out_width = 4 * cols - out_start
    if out_width % 128 or out_start % out_width:
        out_start, out_width = 0, 4 * cols
    out_w = (attn_w[0], (out_width, out_start // out_width))
    out_skip = 3 * cols - out_start
    down_w = gather_weight(down_weight.T)
    grad_mlp = gate_two * grad_out
    grad_mlp_low = grad_mlp.astype(BF)

    normed_ctx, inverse_ctx = normalize(context.astype(F32))
    hidden_ctx = (normed_ctx * (1.0 + scale_one) + shift_one).astype(BF)
    normed_one, inverse_one, hidden_one = normed_ctx[:rows], inverse_ctx[:rows], hidden_ctx[:rows]
    residual = latents_in.astype(F32)
    hidden_t, grad_mlp_t = transposed(order, hidden_ctx, grad_mlp_low)
    queries, keys_ctx, values_ctx = project_qkv(
        order, hidden_ctx, rows, attn_w, query_bias_all, value_bias_all
    )
    mixed, log_sums, head_tops = attend(order, queries, keys_ctx, values_ctx)
    head_tops = jnp.max(head_tops, axis=2)
    attn_out = project_back(order, [mixed], out_w, [out_skip]) + out_bias_all
    after_attn = residual + gate_one * attn_out
    normed_two, inverse_two = normalize(after_attn)
    hidden_two = (normed_two * (1.0 + scale_two) + shift_two).astype(BF)
    activation, gelu_slope = project_up(order, hidden_two, up_w, up_bias_all)
    sum_down = Exchange(scatter_steps(order, [grad_mlp_t], [0], [activation]))
    grad_up_low, up_sums = project_act_back(order, grad_mlp_low, down_w, gelu_slope)
    order.tick(sum_down)
    sum_up = Exchange(scatter_steps(order, [hidden_two.T], [0], [grad_up_low]))
    grad_hidden_two = project_back(order, [grad_up_low], up_w, [0])
    mlp_out = project_back(order, [activation], down_w, [0]) + down_bias_all
    order.tick(sum_down, sum_up)
    block_out = after_attn + gate_two * mlp_out
    grad_after = grad_out + normalize_back(
        grad_hidden_two * (1.0 + scale_two), normed_two, inverse_two
    )
    grad_attn = gate_one * grad_after
    grad_attn_low = grad_attn.astype(BF)
    grad_mixed_low = project_mixed_back(order, grad_attn_low, out_w, cols, out_skip)
    grad_attn_t = grad_attn_low.T
    tops_row = jnp.zeros((1, width), F32).at[0, : size_gy * heads_here].set(head_tops.reshape(-1))
    early = Exchange(
        total_steps(
            jnp.concatenate(
                [rows_sum(grad_mlp), rows_sum(grad_attn), up_sums.reshape(-1, width), tops_row],
                axis=0,
            )
        )
    )

    half = (heads_here + 1) // 2
    head_sets = [x for x in (range(half), range(half, heads_here)) if len(x)]
    sum_attn, back_parts, grad_ctx = [], [], None
    grad_low = None
    for i, heads in enumerate(head_sets):
        parts = attend_back(
            order, queries, keys_ctx, values_ctx, mixed, grad_mixed_low, log_sums, heads
        )
        back_parts.append(parts)
        extra, last = i == 0, i + 1 == len(head_sets)
        sum_new = Exchange(
            scatter_steps(
                order,
                [hidden_t] + [grad_attn_t] * extra,
                [0, 0, 0] + [1] * extra,
                list(parts) + [mixed] * extra,
            )
        )
        order.tick(early, sum_down, sum_up, *sum_attn)
        sum_attn.append(sum_new)
        start = heads[0] * HD
        grad_ctx = project_back(
            order,
            list(parts),
            attn_w,
            [start, cols + start, 2 * cols + start],
            grad_ctx,
            rows if last and span > 1 else None,
        )
        if last and span > 1:
            grad_low, grad_ctx = grad_ctx
        order.tick(early, sum_down, sum_up, *sum_attn)
    grad_hidden_one = grad_ctx[:rows]
    order.token, grad_low = lax.optimization_barrier((order.token, grad_low))
    backs = [
        lax.ppermute(
            grad_low[(s - 1) * rows : s * rows], "gx", [(b, a) for a, b in shift_pairs(s)]
        )
        for s in range(1, span)
    ]
    for back in backs:
        grad_hidden_one += back.astype(F32)
    grad_input = grad_after + normalize_back(
        grad_hidden_one * (1.0 + scale_one), normed_one, inverse_one
    )

    def group_sum(i):
        return jnp.concatenate(
            [jnp.sum(x[i].astype(F32), axis=1) for x in back_parts], axis=1
        ).reshape(1, width)

    late = jnp.concatenate(
        [
            rows_sum(grad_hidden_one),
            rows_sum(grad_hidden_one * normed_one),
            rows_sum(grad_after * attn_out),
            rows_sum(grad_hidden_two),
            rows_sum(grad_hidden_two * normed_two),
            rows_sum(grad_out * mlp_out),
            group_sum(0),
            group_sum(2),
        ],
        axis=0,
    )
    late += order.token[:1, :1]
    for bit in bits_of("gx"):
        if bit < span:
            late = late + swap(late, "gx", bit)
    late = late.astype(BF)[None]
    for axis in ("gx", "gy"):
        for bit in bits_of(axis):
            if axis == "gy" or bit >= span:
                late = jnp.concatenate([late, swap(late, axis, bit)], axis=0)
    late_all = jnp.concatenate([late, swap(late, "dp", 1)], axis=0)
    at_latent = at_gy * (size_gx // span) + at_gx // span
    grad_ada_b = jnp.sum(late_all[:, :6].astype(F32), axis=0)
    tail_sum = jnp.sum(late_all[:, 6:].astype(F32), axis=0)
    grad_query_b = lax.dynamic_slice_in_dim(tail_sum[0], at_gy * cols, cols, 0)
    grad_value_b = lax.dynamic_slice_in_dim(tail_sum[1], at_gy * cols, cols, 0)
    silu_near = by_distance(silu_cond, at_latent)
    silu_every = jnp.concatenate(
        [silu_near, by_distance(swap(silu_cond, "dp", 1), at_latent)], axis=0
    )
    grad_ada_w = dot("le,lmf->emf", silu_every, late_all[:, :6])
    grad_silu = by_distance(dot("lmf,emf->le", late[:, :6], ada_weight), at_latent)
    sigmoid_cond = jax.nn.sigmoid(cond_f32)
    grad_condition = grad_silu * sigmoid_cond * (1.0 + cond_f32 * (1.0 - sigmoid_cond))

    early_sum = early.result()
    grad_down_b = lax.dynamic_slice_in_dim(early_sum[0], at_gx * width_x, width_x, 0)
    grad_out_b = lax.dynamic_slice_in_dim(early_sum[1], at_gx * width_x, width_x, 0)
    grad_up_b = lax.dynamic_slice_in_dim(early_sum[2:-1].reshape(-1), at_gy * up_cols, up_cols, 0)
    logit_max = lax.dynamic_slice_in_dim(early_sum[-1], at_gy * heads_here, heads_here, 0)

    grad_down_w, grad_up_w = sum_down.result(), sum_up.result()
    sums = [x.result() for x in sum_attn]
    grad_qkv = [
        jnp.concatenate(
            [x[:, i * HD * len(h) : (i + 1) * HD * len(h)] for x, h in zip(sums, head_sets)], axis=1
        )
        for i in range(3)
    ]
    out_at = 3 * HD * len(head_sets[0])
    grad_out_w = sums[0][:, out_at : out_at + cols]

    factor = TAU / jnp.maximum(logit_max, TAU)
    root_cols = jnp.repeat(jnp.sqrt(factor), HD)
    clipped_query = query_weight.astype(F32) * root_cols[None, :]
    clipped_key = key_weight.astype(F32) * root_cols[None, :]
    clipped_bias = query_bias * root_cols
    return (
        block_out,
        grad_input,
        grad_condition,
        grad_ada_w,
        grad_ada_b,
        *grad_qkv,
        grad_query_b,
        grad_value_b,
        grad_out_w.T,
        grad_out_b,
        grad_up_w,
        grad_up_b,
        grad_down_w.T,
        grad_down_b,
        logit_max,
        clipped_query,
        clipped_key,
        clipped_bias,
    )


def solution(mesh):
    placed = (
        P(("dp", "gy", "gx"), None),
        P("dp", "gy"),
        P("gy", None, None),
        P(),
        P("gx", "gy"),
        P("gx", "gy"),
        P("gx", "gy"),
        P("gy"),
        P("gy"),
        P("gy", "gx"),
        P("gx"),
        P("gx", "gy"),
        P("gy"),
        P("gy", "gx"),
        P("gx"),
        P(("dp", "gy", "gx"), None),
    )
    return jax.shard_map(
        body,
        mesh=mesh,
        in_specs=placed,
        out_specs=(
            P(("dp", "gy", "gx"), None),
            P(("dp", "gy", "gx"), None),
            P("dp", "gy"),
            P("gy", None, None),
            P(),
            P("gx", "gy"),
            P("gx", "gy"),
            P("gx", "gy"),
            P("gy"),
            P("gy"),
            P("gy", "gx"),
            P("gx"),
            P("gx", "gy"),
            P("gy"),
            P("gy", "gx"),
            P("gx"),
            P("gy"),
            P("gx", "gy"),
            P("gx", "gy"),
            P("gy"),
        ),
        check_vma=False,
    )
```

```python
import math

import jax
import jax.numpy as jnp
from jax import lax
from jax.experimental import pallas as pl
from jax.experimental.pallas import tpu as pltpu
from jax.sharding import PartitionSpec as P

HD = 72
SEQ = 1024
TAU = 8

EPS = 1e-06
GELU_ROOT = 0.7978845608028654
GELU_CUBE = 0.044715
BF = jnp.bfloat16
F32 = jnp.float32
EVERY = ("gy", "gx", "dp")


def gelu_parts(inputs):
    inner_arg = GELU_ROOT * (inputs + GELU_CUBE * inputs * inputs * inputs)
    tangent = jnp.tanh(inner_arg)
    output = 0.5 * inputs * (1.0 + tangent)
    slope_rows = 0.5 * (1.0 + tangent) + 0.5 * inputs * (1.0 - tangent * tangent) * GELU_ROOT * (
        1.0 + 3.0 * GELU_CUBE * inputs * inputs
    )
    return (output, slope_rows)


def normalize(rows_in):
    mean_row = jnp.mean(rows_in, axis=1, keepdims=True)
    centred = rows_in - mean_row
    inverse = lax.rsqrt(jnp.mean(centred * centred, axis=1, keepdims=True) + EPS)
    return (centred * inverse, inverse)


def normalize_back(grad_hat, normed, inverse):
    grad_mean = jnp.mean(grad_hat, axis=1, keepdims=True)
    cross_mean = jnp.mean(grad_hat * normed, axis=1, keepdims=True)
    return inverse * (grad_hat - grad_mean - normed * cross_mean)


def swap(values, axis, bit):
    pairs = [(i, i ^ bit) for i in range(lax.axis_size(axis))]
    return lax.ppermute(values, axis, pairs)


def bits_of(axis):
    return [1 << k for k in range(lax.axis_size(axis).bit_length() - 1)]


def cube_gather(values, axis):
    at = lax.axis_index(axis)
    for bit in bits_of(axis):
        other = swap(values, axis, bit)
        low = (at & bit) == 0
        values = jnp.concatenate(
            [jnp.where(low, values, other), jnp.where(low, other, values)], axis=0
        )
    return values


def by_distance(values, index):
    count = values.shape[0]
    for k in range(count.bit_length() - 1):
        pairs = values.reshape((-1, 2, 1 << k) + values.shape[1:])
        flipped = jnp.concatenate([pairs[:, 1:], pairs[:, :1]], axis=1).reshape(values.shape)
        values = jnp.where((index >> k) & 1 == 1, flipped, values)
    return values


def total_steps(values):
    summed = lax.broadcasted_iota(jnp.int32, values.shape, 0) < values.shape[0] - 1
    for axis in ("dp", "gx", "gy"):
        for bit in bits_of(axis):
            values, got = yield (values, swap(values, axis, bit))
            values = jnp.where(summed, values + got, jnp.maximum(values, got))
    yield values


def pick(values, index, axis=0):
    return lax.dynamic_index_in_dim(values, index, axis, keepdims=False)


def add_low(left, right):
    return (left.astype(F32) + right.astype(F32)).astype(BF)


def own_half(shard):
    part = shard.shape[0] // 2
    return lax.dynamic_slice_in_dim(shard, lax.axis_index("dp") * part, part, 0)


def gather_weight(shard):
    full = lax.all_gather(own_half(shard), EVERY, axis=0, tiled=True)
    return full.reshape(lax.axis_size("gy"), -1, shard.shape[1])


def cube_mesh():
    return (lax.axis_size("gy"), lax.axis_size("gx"), lax.axis_size("dp")) == (4, 4, 2)


def scatter_steps(order, lefts, picks, rights):
    size_gx = lax.axis_size("gx")
    at_gy, at_gx, at_dp = lax.axis_index("gy"), lax.axis_index("gx"), lax.axis_index("dp")
    if cube_mesh():
        other = weight_grads_near(order, lefts, picks, rights, 1 - at_dp)
        (got,) = yield (swap(other, "dp", 1),)
        one, send_one, two, send_two = weight_grads_near(order, lefts, picks, rights, at_dp, got)
        one, two, got_one, got_two = yield (
            one,
            two,
            swap(send_one, "gy", 1),
            swap(send_two, "gy", 2),
        )
        one, two, got_one, got_two = yield (
            add_low(one[0], got_one[0]),
            add_low(two[0], got_two[0]),
            swap(add_low(one[1], got_one[1]), "gy", 2),
            swap(add_low(two[1], got_two[1]), "gy", 1),
        )
        at_z1, at_z0 = at_gx // 2, at_gx % 2
        acc = jnp.stack([add_low(one, got_one), add_low(two, got_two)])
        acc = acc.reshape(2, 2, -1, acc.shape[2])
        acc, got = yield (pick(acc, at_z0, 1), swap(pick(acc, 1 - at_z0, 1), "gx", 1))
        acc = add_low(acc, got)
        acc, got = yield (pick(acc, at_z1), swap(pick(acc, 1 - at_z1), "gx", 2))
        acc = add_low(acc, got)
    else:
        other, mine = [
            weight_grads(order, [half_rows(x, w) for x in lefts], picks, rights)
            for w in (1 - at_dp, at_dp)
        ]
        got, mine = yield (swap(other, "dp", 1), mine)
        acc = add_low(mine, got)
        acc = lax.psum_scatter(
            acc.reshape(-1, acc.shape[2]), ("gy", "gx"), scatter_dimension=0, tiled=True
        )
    acc, got = yield (acc, swap(acc, "dp", 1))
    low = at_dp == 0
    yield jnp.concatenate([jnp.where(low, acc, got), jnp.where(low, got, acc)], axis=0).astype(F32)


class Exchange:
    def __init__(self, steps):
        self.steps = steps
        self.state = next(self.steps)
        self.done = not isinstance(self.state, tuple)

    def advance(self):
        self.state = self.steps.send(self.state)
        self.done = not isinstance(self.state, tuple)

    def result(self):
        while not self.done:
            self.advance()
        return self.state


class Order:
    def __init__(self):
        self.token = jnp.zeros((8, 128), F32)

    def tick(self, *exchanges):
        live = [x for x in exchanges if not x.done]
        self.token, states = lax.optimization_barrier((self.token, [x.state for x in live]))
        for x, state in zip(live, states):
            x.state = state
            x.advance()


ORDER_SPEC = pl.BlockSpec((8, 128), lambda *_: (0, 0))
ORDER_SHAPE = jax.ShapeDtypeStruct((8, 128), F32)


def half_rows(values, which):
    width, rows = values.shape
    blocks = values.reshape(lax.axis_size("gx"), 2, -1, rows)
    return pick(blocks, which, 1).reshape(width // 2, rows)


LOG2E = 1.4426950408889634
SCALE = 1.0 / math.sqrt(HD)


def dot(spec, left, right):
    return jnp.einsum(spec, left, right, preferred_element_type=F32)


def dot_t(left, right):
    return lax.dot_general(left, right, (((1,), (1,)), ((), ())), preferred_element_type=F32)


def dot_n(left, right):
    return jnp.dot(left, right, preferred_element_type=F32)


def by_group(order, kernel, name, whole, grouped, outs, flops, whole_outs=(), scratch=()):
    parts = [x[1] if isinstance(x, tuple) else (x.shape[2], 0) for x in grouped]
    grouped = [x[0] if isinstance(x, tuple) else x for x in grouped]
    g = grouped[0].shape[0]

    def block(rows, cols, k=0):
        return pl.BlockSpec((1, rows, cols), lambda i: (i, 0, k))

    def in_order(order_ref, *refs):
        inputs = len(whole) + len(grouped)
        refs[inputs][...] = order_ref[...]
        kernel(*refs[:inputs], *refs[inputs + 1 :])

    shapes = [jax.ShapeDtypeStruct((g,) + shape, kind) for shape, kind in outs]
    specs = [block(*x.shape[1:]) for x in shapes]
    for shape, kind in whole_outs:
        shapes.append(jax.ShapeDtypeStruct(shape, kind))
        specs.append(pl.BlockSpec(shape, lambda i: (0, 0)))
    moved = sum(x.size * x.dtype.itemsize for x in [*whole, *grouped, *shapes])
    order.token, *results = pl.pallas_call(
        in_order,
        out_shape=[ORDER_SHAPE, *shapes],
        grid=(g,),
        in_specs=[ORDER_SPEC]
        + [pl.BlockSpec(x.shape, lambda i: (0, 0)) for x in whole]
        + [block(x.shape[1], *part) for x, part in zip(grouped, parts)],
        out_specs=[ORDER_SPEC, *specs],
        scratch_shapes=scratch,
        cost_estimate=pl.CostEstimate(flops=flops * g, transcendentals=0, bytes_accessed=moved),
        name=name,
    )(order.token, *whole, *grouped)
    return results


def transposed(order, *arrays):
    count = len(arrays)

    def kernel(order_ref, *refs):
        refs[count][...] = order_ref[...]
        for x_ref, out_ref in zip(refs[:count], refs[count + 1 :]):
            out_ref[...] = x_ref[...].T

    order.token, *results = pl.pallas_call(
        kernel,
        out_shape=[ORDER_SHAPE, *[jax.ShapeDtypeStruct(x.shape[::-1], BF) for x in arrays]],
        name="transposed",
    )(order.token, *arrays)
    return results


def edges_of(rights):
    edges = [0]
    for right in rights:
        edges.append(edges[-1] + right.shape[2])
    return edges


def weight_grads(order, lefts, picks, rights):
    m, edges = lefts[0].shape[0], edges_of(rights)

    def kernel(*refs):
        for i, k in enumerate(picks):
            right = refs[len(lefts) + i][0]
            refs[-1][0, :, edges[i] : edges[i + 1]] = dot_n(
                refs[k][:, : right.shape[0]], right
            ).astype(BF)

    flops = sum(2 * m * x.shape[1] * x.shape[2] for x in rights)
    return by_group(order, kernel, "weight_grads", lefts, rights, [((m, edges[-1]), BF)], flops)[0]


def weight_grads_near(order, lefts, picks, rights, side, got=None):
    size_gx = lax.axis_size("gx")
    lefts = [x.reshape(size_gx, 2, -1, x.shape[1]) for x in lefts]
    m, edges = size_gx * lefts[0].shape[2], edges_of(rights)
    n, part = -(-edges[-1] // 128) * 128, m // 2

    def kernel(place_ref, order_ref, *refs):
        left_refs, right_refs = refs[: len(lefts)], refs[len(lefts) : len(lefts) + len(rights)]
        rest = refs[len(lefts) + len(rights) :]
        if got is not None:
            got_ref, rest = rest[0], rest[1:]
        step = pl.program_id(0)
        rest[0][...] = order_ref[...]
        rest = rest[1:]

        def product(i):
            right = right_refs[i][0]
            left = left_refs[picks[i]][:, 0, :, : right.shape[0]]
            return dot_n(left.reshape(m, right.shape[0]), right)

        if got is None:
            for i in range(len(rights)):
                rest[0][0, :, edges[i] : edges[i + 1]] = product(i).astype(BF)
            if n > edges[-1]:
                rest[0][0, :, edges[-1] :] = jnp.zeros((m, n - edges[-1]), BF)
            return
        one_ref, send_one_ref, two_ref, send_two_ref, sum_ref = rest
        for i in range(len(rights)):
            at = slice(edges[i], edges[i + 1])
            sum_ref[:, at] = (product(i) + got_ref[0, :, at].astype(F32)).astype(BF)
        if n > edges[-1]:
            sum_ref[:, edges[-1] :] = jnp.zeros((m, n - edges[-1]), BF)

        for ref, rows, wanted in (
            (one_ref, slice(0, part), step % 2 == 0),
            (send_one_ref, slice(0, part), step % 2 == 1),
            (two_ref, slice(part, m), step // 2 == 0),
            (send_two_ref, slice(part, m), step // 2 == 1),
        ):

            @pl.when(wanted)
            def _(ref=ref, rows=rows):
                ref[0] = sum_ref[rows, :]

    place = jnp.stack([side, lax.axis_index("gy")]).astype(jnp.int32)
    in_specs = [ORDER_SPEC] + [
        pl.BlockSpec((size_gx, 1) + x.shape[2:], lambda i, p: (0, p[0], 0, 0)) for x in lefts
    ] + [pl.BlockSpec((1,) + x.shape[1:], lambda i, p: (i ^ p[1], 0, 0)) for x in rights]
    operands = [order.token, *lefts, *rights]
    scratch = []
    if got is None:
        shapes = [jax.ShapeDtypeStruct((4, m, n), BF)]
        out_specs = [pl.BlockSpec((1, m, n), lambda i, p: (i, 0, 0))]
    else:
        operands.append(got)
        in_specs.append(pl.BlockSpec((1, m, n), lambda i, p: (i, 0, 0)))
        shapes = [jax.ShapeDtypeStruct((2, part, n), BF)] * 4
        out_specs = [
            pl.BlockSpec((1, part, n), lambda i, p: (i // 2, 0, 0)),
            pl.BlockSpec((1, part, n), lambda i, p: (i // 2, 0, 0)),
            pl.BlockSpec((1, part, n), lambda i, p: (jnp.minimum(i, 1), 0, 0)),
            pl.BlockSpec((1, part, n), lambda i, p: (jnp.maximum(i, 2) - 2, 0, 0)),
        ]
        scratch = [pltpu.VMEM((m, n), BF)]
    flops = sum(8 * m * x.shape[1] * x.shape[2] for x in rights)
    moved = 8 * m * n * (1 if got is None else 2) + sum(2 * x.size for x in rights)
    order.token, *results = pl.pallas_call(
        kernel,
        out_shape=[ORDER_SHAPE, *shapes],
        grid_spec=pltpu.PrefetchScalarGridSpec(
            num_scalar_prefetch=1,
            grid=(4,),
            in_specs=in_specs,
            out_specs=[ORDER_SPEC, *out_specs],
            scratch_shapes=scratch,
        ),
        cost_estimate=pl.CostEstimate(flops=flops, transcendentals=0, bytes_accessed=moved),
        name="weight_grads_near",
    )(place, *operands)
    return results[0] if got is None else results


def project_back(order, xs, weight, terms, init=None, own=None):
    weight, (w_cols, part) = weight if isinstance(weight, tuple) else (weight, (weight.shape[2], 0))
    width = weight.shape[1]
    rows = xs[0].shape[1] if init is None else init.shape[0]
    rows = max([rows] + [x.shape[1] for x in xs])
    windows = []
    for x, start in zip(xs, terms):
        low = start // 128 * 128
        windows.append((low, min(-(-(start + x.shape[2]) // 128) * 128, w_cols), start - low))
    padded = [w[1] - w[0] != x.shape[2] for x, w in zip(xs, windows)]
    whole = [] if init is None else [init]

    def kernel(*refs):
        refs = list(refs)
        init_ref = refs.pop(0) if whole else None
        x_refs, w_ref = refs[: len(xs)], refs[len(xs)]
        refs = refs[len(xs) + 1 :]
        low_ref = refs.pop(0) if own is not None else None
        out_ref, wide_refs = refs[0], refs[1:]

        @pl.when(pl.program_id(0) == 0)
        def _():
            out_ref[...] = jnp.zeros((rows, width), F32) if init_ref is None else init_ref[...]
            for ref in wide_refs:
                ref[...] = jnp.zeros(ref.shape, BF)

        parts, wide = {}, 0
        for x_ref, (low, high, shift), pad in zip(x_refs, windows, padded):
            r, n = x_ref.shape[1:]
            if pad:
                ref = wide_refs[wide]
                wide += 1
                ref[:, shift : shift + n] = x_ref[0]
                x = ref[...]
            else:
                x = x_ref[0]
            part = dot_t(x, w_ref[0, :, low:high])
            parts[r] = parts[r] + part if r in parts else part
        for r, part in parts.items():
            out_ref[:r] += part
        if low_ref is not None:

            @pl.when(pl.program_id(0) == pl.num_programs(0) - 1)
            def _():
                low_ref[...] = out_ref[own:].astype(BF)

    scratch = [
        pltpu.VMEM((x.shape[1], w[1] - w[0]), BF) for x, w, pad in zip(xs, windows, padded) if pad
    ]
    flops = sum(2 * x.shape[1] * width * x.shape[2] for x in xs)
    wholes = [] if own is None else [((rows - own, width), BF)]
    wholes.append(((rows, width), F32))
    results = by_group(
        order,
        kernel,
        "project_back",
        whole,
        [*xs, (weight, (w_cols, part))],
        [],
        flops,
        wholes,
        scratch,
    )
    return results[0] if own is None else results


def project_qkv(order, hidden, rows, weight, bias_q, bias_v):
    ctx, width = hidden.shape
    n = bias_q.shape[2]

    def kernel(h_ref, w_ref, bq_ref, bv_ref, q_ref, k_ref, v_ref):
        joint = dot_n(h_ref[...], w_ref[0, :, : 3 * n])
        q_ref[0] = (joint[:rows, :n] + bq_ref[0]).astype(BF)
        k_ref[0] = joint[:, n : 2 * n].astype(BF)
        v_ref[0] = (joint[:, 2 * n :] + bv_ref[0]).astype(BF)

    return by_group(
        order,
        kernel,
        "project_qkv",
        [hidden],
        [weight, bias_q, bias_v],
        [((rows, n), BF), ((ctx, n), BF), ((ctx, n), BF)],
        6 * ctx * width * n,
    )


def project_up(order, hidden, weight, bias):
    rows, width = hidden.shape
    n = bias.shape[2]

    def kernel(h_ref, w_ref, bias_ref, act_ref, slope_ref):
        activ, slope = gelu_parts(dot_n(h_ref[...], w_ref[0]) + bias_ref[0])
        act_ref[0] = activ.astype(BF)
        slope_ref[0] = slope.astype(BF)

    return by_group(
        order,
        kernel,
        "project_up",
        [hidden],
        [weight, bias],
        [((rows, n), BF), ((rows, n), BF)],
        2 * rows * width * n,
    )


def project_act_back(order, grad_mlp, weight, slope):
    rows, width = grad_mlp.shape
    n = slope.shape[2]

    def kernel(g_ref, w_ref, slope_ref, low_ref, sums_ref):
        grad = dot_n(g_ref[...], w_ref[0]) * slope_ref[0].astype(F32)
        low_ref[0] = grad.astype(BF)
        sums_ref[0] = jnp.sum(grad, axis=0, keepdims=True)

    return by_group(
        order,
        kernel,
        "project_act_back",
        [grad_mlp],
        [weight, slope],
        [((rows, n), BF), ((1, n), F32)],
        2 * rows * width * n,
    )


def project_mixed_back(order, grad_attn, weight, n, skip):
    rows, width = grad_attn.shape

    def kernel(g_ref, w_ref, out_ref):
        out_ref[0] = dot_n(g_ref[...], w_ref[0])[:, skip:].astype(BF)

    return by_group(
        order,
        kernel,
        "project_mixed_back",
        [grad_attn],
        [weight],
        [((rows, n), BF)],
        2 * rows * width * n,
    )[0]


def head_of(ref, h):
    return ref[0, :, h * HD : (h + 1) * HD]


def attend(order, queries, keys_ctx, values_ctx):
    _, rows, n = queries.shape
    ctx = keys_ctx.shape[1]
    heads = n // HD

    def kernel(q_ref, k_ref, v_ref, mixed_ref, sums_ref, tops_ref):
        for h in range(heads):
            q, k, v = head_of(q_ref, h), head_of(k_ref, h), head_of(v_ref, h)
            scores = dot_t(k, q)
            top = jnp.max(scores, axis=0, keepdims=True)
            weights = jnp.exp2((scores - top) * (SCALE * LOG2E))
            total = jnp.sum(weights, axis=0, keepdims=True)
            mixed = dot_n(v.T, weights.astype(BF)) / total
            mixed_ref[0, :, h * HD : (h + 1) * HD] = mixed.T.astype(BF)
            sums_ref[0, h : h + 1, :] = top * (SCALE * LOG2E) + jnp.log2(total)
            tops_ref[0, h : h + 1, :] = top * SCALE

    return by_group(
        order,
        kernel,
        "attend",
        [],
        [queries, keys_ctx, values_ctx],
        [((rows, n), BF), ((heads, rows), F32), ((heads, rows), F32)],
        14 * rows * ctx * n,
    )


def attend_back(order, queries, keys_ctx, values_ctx, mixed, grad_mixed, log_sums, heads):
    _, rows, n = queries.shape
    ctx = keys_ctx.shape[1]
    n_out = len(heads) * HD

    def kernel(q_ref, k_ref, v_ref, x_ref, g_ref, sums_ref, gq_ref, gk_ref, gv_ref):
        for j, h in enumerate(heads):
            q, k, v = head_of(q_ref, h), head_of(k_ref, h), head_of(v_ref, h)
            grad = head_of(g_ref, h)
            delta = jnp.sum(
                (head_of(x_ref, h).astype(F32) * grad.astype(F32)).T, axis=0, keepdims=True
            )
            probs = jnp.exp2(dot_t(k, q) * (SCALE * LOG2E) - sums_ref[0, h : h + 1, :])
            grad_scores = (probs * (dot_t(v, grad) - delta)).astype(BF)
            out = slice(j * HD, (j + 1) * HD)
            gk_ref[0, :, out] = (dot_n(grad_scores, q) * SCALE).astype(BF)
            gv_ref[0, :, out] = dot_n(probs.astype(BF), grad).astype(BF)
            gq_ref[0, :, out] = (dot_n(k.T, grad_scores) * SCALE).T.astype(BF)

    return by_group(
        order,
        kernel,
        "attend_back",
        [],
        [queries, keys_ctx, values_ctx, mixed, grad_mixed, log_sums],
        [((rows, n_out), BF), ((ctx, n_out), BF), ((ctx, n_out), BF)],
        35 * rows * ctx * n_out,
    )


def body(
    latents_in,
    condition,
    ada_weight,
    ada_bias,
    query_weight,
    key_weight,
    value_weight,
    query_bias,
    value_bias,
    out_weight,
    out_bias,
    up_weight,
    up_bias,
    down_weight,
    down_bias,
    grad_out,
):
    rows, width = latents_in.shape
    latent_count = condition.shape[0]
    cols = query_weight.shape[1]
    width_x = out_bias.shape[0]
    size_gx, size_gy = lax.axis_size("gx"), lax.axis_size("gy")
    at_gx, at_gy = lax.axis_index("gx"), lax.axis_index("gy")
    span = SEQ // rows
    heads_here = cols // HD

    def rows_sum(values):
        return jnp.sum(values, axis=-2).reshape(-1, width)

    def shift_pairs(shift):
        return [(i, i // span * span + (i + shift) % span) for i in range(size_gx)]

    context = jnp.concatenate(
        [latents_in] + [lax.ppermute(latents_in, "gx", shift_pairs(s)) for s in range(1, span)], axis=0
    )

    cond_f32 = condition.astype(F32)
    silu_cond = jax.nn.silu(cond_f32).astype(BF)
    mod_part = dot("le,emf->lmf", silu_cond, ada_weight)
    for bit in reversed(bits_of("gy")):
        mod_pair = mod_part.reshape((2, -1) + mod_part.shape[1:])
        side = (at_gy // bit) % 2
        mod_part = pick(mod_pair, side) + swap(pick(mod_pair, 1 - side), "gy", bit)
    mod_own = pick(mod_part, at_gx // span) + ada_bias
    shift_one, scale_one, gate_one, shift_two, scale_two, gate_two = [
        mod_own[m : m + 1] for m in range(6)
    ]

    along_x = cube_gather(jnp.concatenate([out_bias, down_bias])[None], "gx")
    out_bias_all = along_x[:, :width_x].reshape(1, width)
    down_bias_all = along_x[:, width_x:].reshape(1, width)
    rest = cube_gather(jnp.concatenate([query_bias, value_bias, up_bias])[None], "gy")
    query_bias_all = rest[:, None, :cols]
    value_bias_all = rest[:, None, cols : 2 * cols]
    up_bias_all = rest[:, None, 2 * cols :]

    order = Order()
    up_cols = up_bias.shape[0]
    attn_part = jnp.concatenate([query_weight, key_weight, value_weight, out_weight.T], axis=1)
    if up_cols == 4 * cols and up_cols % 128 == 0:
        joint_w = gather_weight(jnp.concatenate([attn_part, up_weight], axis=1))
        attn_w, up_w = (joint_w, (up_cols, 0)), (joint_w, (up_cols, 1))
    else:
        attn_w = (gather_weight(attn_part), (4 * cols, 0))
        up_w = (gather_weight(up_weight), (up_cols, 0))
    out_start = 3 * cols // 128 * 128
    out_width = 4 * cols - out_start
    if out_width % 128 or out_start % out_width:
        out_start, out_width = 0, 4 * cols
    out_w = (attn_w[0], (out_width, out_start // out_width))
    out_skip = 3 * cols - out_start
    down_w = gather_weight(down_weight.T)
    grad_mlp = gate_two * grad_out
    grad_mlp_low = grad_mlp.astype(BF)

    normed_ctx, inverse_ctx = normalize(context.astype(F32))
    hidden_ctx = (normed_ctx * (1.0 + scale_one) + shift_one).astype(BF)
    normed_one, inverse_one, hidden_one = normed_ctx[:rows], inverse_ctx[:rows], hidden_ctx[:rows]
    residual = latents_in.astype(F32)
    hidden_t, grad_mlp_t = transposed(order, hidden_ctx, grad_mlp_low)
    queries, keys_ctx, values_ctx = project_qkv(
        order, hidden_ctx, rows, attn_w, query_bias_all, value_bias_all
    )
    mixed, log_sums, head_tops = attend(order, queries, keys_ctx, values_ctx)
    head_tops = jnp.max(head_tops, axis=2)
    attn_out = project_back(order, [mixed], out_w, [out_skip]) + out_bias_all
    after_attn = residual + gate_one * attn_out
    normed_two, inverse_two = normalize(after_attn)
    hidden_two = (normed_two * (1.0 + scale_two) + shift_two).astype(BF)
    activation, gelu_slope = project_up(order, hidden_two, up_w, up_bias_all)
    sum_down = Exchange(scatter_steps(order, [grad_mlp_t], [0], [activation]))
    order.tick(sum_down)
    grad_up_low, up_sums = project_act_back(order, grad_mlp_low, down_w, gelu_slope)
    sum_up = Exchange(scatter_steps(order, [hidden_two.T], [0], [grad_up_low]))
    grad_hidden_two = project_back(order, [grad_up_low], up_w, [0])
    mlp_out = project_back(order, [activation], down_w, [0]) + down_bias_all
    order.tick(sum_down, sum_up)
    block_out = after_attn + gate_two * mlp_out
    grad_after = grad_out + normalize_back(
        grad_hidden_two * (1.0 + scale_two), normed_two, inverse_two
    )
    grad_attn = gate_one * grad_after
    grad_attn_low = grad_attn.astype(BF)
    grad_mixed_low = project_mixed_back(order, grad_attn_low, out_w, cols, out_skip)
    grad_attn_t = grad_attn_low.T
    tops_row = jnp.zeros((1, width), F32).at[0, : size_gy * heads_here].set(head_tops.reshape(-1))
    early = Exchange(
        total_steps(
            jnp.concatenate(
                [rows_sum(grad_mlp), rows_sum(grad_attn), up_sums.reshape(-1, width), tops_row],
                axis=0,
            )
        )
    )

    half = (heads_here + 1) // 2
    head_sets = [x for x in (range(half), range(half, heads_here)) if len(x)]
    sum_attn, back_parts, grad_ctx = [], [], None
    grad_low = None
    for i, heads in enumerate(head_sets):
        parts = attend_back(
            order, queries, keys_ctx, values_ctx, mixed, grad_mixed_low, log_sums, heads
        )
        back_parts.append(parts)
        extra, last = i == 0, i + 1 == len(head_sets)
        sum_new = Exchange(
            scatter_steps(
                order,
                [hidden_t] + [grad_attn_t] * extra,
                [0, 0, 0] + [1] * extra,
                list(parts) + [mixed] * extra,
            )
        )
        order.tick(early, sum_down, sum_up, *sum_attn)
        sum_attn.append(sum_new)
        start = heads[0] * HD
        grad_ctx = project_back(
            order,
            list(parts),
            attn_w,
            [start, cols + start, 2 * cols + start],
            grad_ctx,
            rows if last and span > 1 else None,
        )
        if last and span > 1:
            grad_low, grad_ctx = grad_ctx
        order.tick(early, sum_down, sum_up, *sum_attn)
    grad_hidden_one = grad_ctx[:rows]
    order.token, grad_low = lax.optimization_barrier((order.token, grad_low))
    backs = [
        lax.ppermute(
            grad_low[(s - 1) * rows : s * rows], "gx", [(b, a) for a, b in shift_pairs(s)]
        )
        for s in range(1, span)
    ]
    for back in backs:
        grad_hidden_one += back.astype(F32)
    grad_input = grad_after + normalize_back(
        grad_hidden_one * (1.0 + scale_one), normed_one, inverse_one
    )

    def group_sum(i):
        return jnp.concatenate(
            [jnp.sum(x[i].astype(F32), axis=1) for x in back_parts], axis=1
        ).reshape(1, width)

    late = jnp.concatenate(
        [
            rows_sum(grad_hidden_one),
            rows_sum(grad_hidden_one * normed_one),
            rows_sum(grad_after * attn_out),
            rows_sum(grad_hidden_two),
            rows_sum(grad_hidden_two * normed_two),
            rows_sum(grad_out * mlp_out),
            group_sum(0),
            group_sum(2),
        ],
        axis=0,
    )
    late += order.token[:1, :1]
    for bit in bits_of("gx"):
        if bit < span:
            late = late + swap(late, "gx", bit)
    late = late.astype(BF)[None]
    for axis in ("gx", "gy"):
        for bit in bits_of(axis):
            if axis == "gy" or bit >= span:
                late = jnp.concatenate([late, swap(late, axis, bit)], axis=0)
    late_all = jnp.concatenate([late, swap(late, "dp", 1)], axis=0)
    at_latent = at_gy * (size_gx // span) + at_gx // span
    grad_ada_b = jnp.sum(late_all[:, :6].astype(F32), axis=0)
    tail_sum = jnp.sum(late_all[:, 6:].astype(F32), axis=0)
    grad_query_b = lax.dynamic_slice_in_dim(tail_sum[0], at_gy * cols, cols, 0)
    grad_value_b = lax.dynamic_slice_in_dim(tail_sum[1], at_gy * cols, cols, 0)
    silu_near = by_distance(silu_cond, at_latent)
    silu_every = jnp.concatenate(
        [silu_near, by_distance(swap(silu_cond, "dp", 1), at_latent)], axis=0
    )
    grad_ada_w = dot("le,lmf->emf", silu_every, late_all[:, :6])
    grad_silu = by_distance(dot("lmf,emf->le", late[:, :6], ada_weight), at_latent)
    sigmoid_cond = jax.nn.sigmoid(cond_f32)
    grad_condition = grad_silu * sigmoid_cond * (1.0 + cond_f32 * (1.0 - sigmoid_cond))

    early_sum = early.result()
    grad_down_b = lax.dynamic_slice_in_dim(early_sum[0], at_gx * width_x, width_x, 0)
    grad_out_b = lax.dynamic_slice_in_dim(early_sum[1], at_gx * width_x, width_x, 0)
    grad_up_b = lax.dynamic_slice_in_dim(early_sum[2:-1].reshape(-1), at_gy * up_cols, up_cols, 0)
    logit_max = lax.dynamic_slice_in_dim(early_sum[-1], at_gy * heads_here, heads_here, 0)

    grad_down_w, grad_up_w = sum_down.result(), sum_up.result()
    sums = [x.result() for x in sum_attn]
    grad_qkv = [
        jnp.concatenate(
            [x[:, i * HD * len(h) : (i + 1) * HD * len(h)] for x, h in zip(sums, head_sets)], axis=1
        )
        for i in range(3)
    ]
    out_at = 3 * HD * len(head_sets[0])
    grad_out_w = sums[0][:, out_at : out_at + cols]

    factor = TAU / jnp.maximum(logit_max, TAU)
    root_cols = jnp.repeat(jnp.sqrt(factor), HD)
    clipped_query = query_weight.astype(F32) * root_cols[None, :]
    clipped_key = key_weight.astype(F32) * root_cols[None, :]
    clipped_bias = query_bias * root_cols
    return (
        block_out,
        grad_input,
        grad_condition,
        grad_ada_w,
        grad_ada_b,
        *grad_qkv,
        grad_query_b,
        grad_value_b,
        grad_out_w.T,
        grad_out_b,
        grad_up_w,
        grad_up_b,
        grad_down_w.T,
        grad_down_b,
        logit_max,
        clipped_query,
        clipped_key,
        clipped_bias,
    )


def solution(mesh):
    placed = (
        P(("dp", "gy", "gx"), None),
        P("dp", "gy"),
        P("gy", None, None),
        P(),
        P("gx", "gy"),
        P("gx", "gy"),
        P("gx", "gy"),
        P("gy"),
        P("gy"),
        P("gy", "gx"),
        P("gx"),
        P("gx", "gy"),
        P("gy"),
        P("gy", "gx"),
        P("gx"),
        P(("dp", "gy", "gx"), None),
    )
    return jax.shard_map(
        body,
        mesh=mesh,
        in_specs=placed,
        out_specs=(
            P(("dp", "gy", "gx"), None),
            P(("dp", "gy", "gx"), None),
            P("dp", "gy"),
            P("gy", None, None),
            P(),
            P("gx", "gy"),
            P("gx", "gy"),
            P("gx", "gy"),
            P("gy"),
            P("gy"),
            P("gy", "gx"),
            P("gx"),
            P("gx", "gy"),
            P("gy"),
            P("gy", "gx"),
            P("gx"),
            P("gy"),
            P("gx", "gy"),
            P("gx", "gy"),
            P("gy"),
        ),
        check_vma=False,
    )
```

```python
import math

import jax
import jax.numpy as jnp
from jax import lax
from jax.experimental import pallas as pl
from jax.experimental.pallas import tpu as pltpu
from jax.sharding import PartitionSpec as P

HD = 72
SEQ = 1024
TAU = 8

EPS = 1e-06
GELU_ROOT = 0.7978845608028654
GELU_CUBE = 0.044715
BF = jnp.bfloat16
F32 = jnp.float32
EVERY = ("gy", "gx", "dp")


def gelu_parts(inputs):
    inner_arg = GELU_ROOT * (inputs + GELU_CUBE * inputs * inputs * inputs)
    tangent = jnp.tanh(inner_arg)
    output = 0.5 * inputs * (1.0 + tangent)
    slope_rows = 0.5 * (1.0 + tangent) + 0.5 * inputs * (1.0 - tangent * tangent) * GELU_ROOT * (
        1.0 + 3.0 * GELU_CUBE * inputs * inputs
    )
    return (output, slope_rows)


def normalize(rows_in):
    mean_row = jnp.mean(rows_in, axis=1, keepdims=True)
    centred = rows_in - mean_row
    inverse = lax.rsqrt(jnp.mean(centred * centred, axis=1, keepdims=True) + EPS)
    return (centred * inverse, inverse)


def normalize_back(grad_hat, normed, inverse):
    grad_mean = jnp.mean(grad_hat, axis=1, keepdims=True)
    cross_mean = jnp.mean(grad_hat * normed, axis=1, keepdims=True)
    return inverse * (grad_hat - grad_mean - normed * cross_mean)


def swap(values, axis, bit):
    pairs = [(i, i ^ bit) for i in range(lax.axis_size(axis))]
    return lax.ppermute(values, axis, pairs)


def bits_of(axis):
    return [1 << k for k in range(lax.axis_size(axis).bit_length() - 1)]


def cube_gather(values, axis):
    at = lax.axis_index(axis)
    for bit in bits_of(axis):
        other = swap(values, axis, bit)
        low = (at & bit) == 0
        values = jnp.concatenate(
            [jnp.where(low, values, other), jnp.where(low, other, values)], axis=0
        )
    return values


def by_distance(values, index):
    count = values.shape[0]
    for k in range(count.bit_length() - 1):
        pairs = values.reshape((-1, 2, 1 << k) + values.shape[1:])
        flipped = jnp.concatenate([pairs[:, 1:], pairs[:, :1]], axis=1).reshape(values.shape)
        values = jnp.where((index >> k) & 1 == 1, flipped, values)
    return values


def total_steps(values):
    summed = lax.broadcasted_iota(jnp.int32, values.shape, 0) < values.shape[0] - 1
    for axis in ("dp", "gx", "gy"):
        for bit in bits_of(axis):
            values, got = yield (values, swap(values, axis, bit))
            values = jnp.where(summed, values + got, jnp.maximum(values, got))
    yield values


def pick(values, index, axis=0):
    return lax.dynamic_index_in_dim(values, index, axis, keepdims=False)


def add_low(left, right):
    return (left.astype(F32) + right.astype(F32)).astype(BF)


def own_half(shard):
    part = shard.shape[0] // 2
    return lax.dynamic_slice_in_dim(shard, lax.axis_index("dp") * part, part, 0)


def gather_weight(shard):
    full = lax.all_gather(own_half(shard), EVERY, axis=0, tiled=True)
    return full.reshape(lax.axis_size("gy"), -1, shard.shape[1])


def cube_mesh():
    return (lax.axis_size("gy"), lax.axis_size("gx"), lax.axis_size("dp")) == (4, 4, 2)


def scatter_steps(order, lefts, picks, rights):
    size_gx = lax.axis_size("gx")
    at_gy, at_gx, at_dp = lax.axis_index("gy"), lax.axis_index("gx"), lax.axis_index("dp")
    if cube_mesh():
        other = weight_grads_near(order, lefts, picks, rights, 1 - at_dp)
        (got,) = yield (swap(other, "dp", 1),)
        one, send_one, two, send_two = weight_grads_near(order, lefts, picks, rights, at_dp, got)
        one, two, got_one, got_two = yield (
            one,
            two,
            swap(send_one, "gy", 1),
            swap(send_two, "gy", 2),
        )
        one, two, got_one, got_two = yield (
            add_low(one[0], got_one[0]),
            add_low(two[0], got_two[0]),
            swap(add_low(one[1], got_one[1]), "gy", 2),
            swap(add_low(two[1], got_two[1]), "gy", 1),
        )
        at_z1, at_z0 = at_gx // 2, at_gx % 2
        acc = jnp.stack([add_low(one, got_one), add_low(two, got_two)])
        acc = acc.reshape(2, 2, -1, acc.shape[2])
        acc, got = yield (pick(acc, at_z0, 1), swap(pick(acc, 1 - at_z0, 1), "gx", 1))
        acc = add_low(acc, got)
        acc, got = yield (pick(acc, at_z1), swap(pick(acc, 1 - at_z1), "gx", 2))
        acc = add_low(acc, got)
    else:
        other, mine = [
            weight_grads(order, [half_rows(x, w) for x in lefts], picks, rights)
            for w in (1 - at_dp, at_dp)
        ]
        got, mine = yield (swap(other, "dp", 1), mine)
        acc = add_low(mine, got)
        acc = lax.psum_scatter(
            acc.reshape(-1, acc.shape[2]), ("gy", "gx"), scatter_dimension=0, tiled=True
        )
    acc, got = yield (acc, swap(acc, "dp", 1))
    low = at_dp == 0
    yield jnp.concatenate([jnp.where(low, acc, got), jnp.where(low, got, acc)], axis=0).astype(F32)


class Exchange:
    def __init__(self, steps):
        self.steps = steps
        self.state = next(self.steps)
        self.done = not isinstance(self.state, tuple)

    def advance(self):
        self.state = self.steps.send(self.state)
        self.done = not isinstance(self.state, tuple)

    def result(self):
        while not self.done:
            self.advance()
        return self.state


class Order:
    def __init__(self):
        self.token = jnp.zeros((8, 128), F32)

    def tick(self, *exchanges):
        live = [x for x in exchanges if not x.done]
        self.token, states = lax.optimization_barrier((self.token, [x.state for x in live]))
        for x, state in zip(live, states):
            x.state = state
            x.advance()


ORDER_SPEC = pl.BlockSpec((8, 128), lambda *_: (0, 0))
ORDER_SHAPE = jax.ShapeDtypeStruct((8, 128), F32)


def half_rows(values, which):
    width, rows = values.shape
    blocks = values.reshape(lax.axis_size("gx"), 2, -1, rows)
    return pick(blocks, which, 1).reshape(width // 2, rows)


LOG2E = 1.4426950408889634
SCALE = 1.0 / math.sqrt(HD)


def dot(spec, left, right):
    return jnp.einsum(spec, left, right, preferred_element_type=F32)


def dot_t(left, right):
    return lax.dot_general(left, right, (((1,), (1,)), ((), ())), preferred_element_type=F32)


def dot_n(left, right):
    return jnp.dot(left, right, preferred_element_type=F32)


def by_group(order, kernel, name, whole, grouped, outs, flops, whole_outs=(), scratch=()):
    parts = [x[1] if isinstance(x, tuple) else (x.shape[2], 0) for x in grouped]
    grouped = [x[0] if isinstance(x, tuple) else x for x in grouped]
    g = grouped[0].shape[0]

    def block(rows, cols, k=0):
        return pl.BlockSpec((1, rows, cols), lambda i: (i, 0, k))

    def in_order(order_ref, *refs):
        inputs = len(whole) + len(grouped)
        refs[inputs][...] = order_ref[...]
        kernel(*refs[:inputs], *refs[inputs + 1 :])

    shapes = [jax.ShapeDtypeStruct((g,) + shape, kind) for shape, kind in outs]
    specs = [block(*x.shape[1:]) for x in shapes]
    for shape, kind in whole_outs:
        shapes.append(jax.ShapeDtypeStruct(shape, kind))
        specs.append(pl.BlockSpec(shape, lambda i: (0, 0)))
    moved = sum(x.size * x.dtype.itemsize for x in [*whole, *grouped, *shapes])
    order.token, *results = pl.pallas_call(
        in_order,
        out_shape=[ORDER_SHAPE, *shapes],
        grid=(g,),
        in_specs=[ORDER_SPEC]
        + [pl.BlockSpec(x.shape, lambda i: (0, 0)) for x in whole]
        + [block(x.shape[1], *part) for x, part in zip(grouped, parts)],
        out_specs=[ORDER_SPEC, *specs],
        scratch_shapes=scratch,
        cost_estimate=pl.CostEstimate(flops=flops * g, transcendentals=0, bytes_accessed=moved),
        name=name,
    )(order.token, *whole, *grouped)
    return results


def transposed(order, *arrays):
    count = len(arrays)

    def kernel(order_ref, *refs):
        refs[count][...] = order_ref[...]
        for x_ref, out_ref in zip(refs[:count], refs[count + 1 :]):
            out_ref[...] = x_ref[...].T

    order.token, *results = pl.pallas_call(
        kernel,
        out_shape=[ORDER_SHAPE, *[jax.ShapeDtypeStruct(x.shape[::-1], BF) for x in arrays]],
        name="transposed",
    )(order.token, *arrays)
    return results


def edges_of(rights):
    edges = [0]
    for right in rights:
        edges.append(edges[-1] + right.shape[2])
    return edges


def weight_grads(order, lefts, picks, rights):
    m, edges = lefts[0].shape[0], edges_of(rights)

    def kernel(*refs):
        for i, k in enumerate(picks):
            right = refs[len(lefts) + i][0]
            refs[-1][0, :, edges[i] : edges[i + 1]] = dot_n(
                refs[k][:, : right.shape[0]], right
            ).astype(BF)

    flops = sum(2 * m * x.shape[1] * x.shape[2] for x in rights)
    return by_group(order, kernel, "weight_grads", lefts, rights, [((m, edges[-1]), BF)], flops)[0]


def weight_grads_near(order, lefts, picks, rights, side, got=None):
    size_gx = lax.axis_size("gx")
    lefts = [x.reshape(size_gx, 2, -1, x.shape[1]) for x in lefts]
    m, edges = size_gx * lefts[0].shape[2], edges_of(rights)
    n, part = -(-edges[-1] // 128) * 128, m // 2

    def kernel(place_ref, order_ref, *refs):
        left_refs, right_refs = refs[: len(lefts)], refs[len(lefts) : len(lefts) + len(rights)]
        rest = refs[len(lefts) + len(rights) :]
        if got is not None:
            got_ref, rest = rest[0], rest[1:]
        step = pl.program_id(0)
        rest[0][...] = order_ref[...]
        rest = rest[1:]

        def product(i):
            right = right_refs[i][0]
            left = left_refs[picks[i]][:, 0, :, : right.shape[0]]
            return dot_n(left.reshape(m, right.shape[0]), right)

        if got is None:
            for i in range(len(rights)):
                rest[0][0, :, edges[i] : edges[i + 1]] = product(i).astype(BF)
            if n > edges[-1]:
                rest[0][0, :, edges[-1] :] = jnp.zeros((m, n - edges[-1]), BF)
            return
        one_ref, send_one_ref, two_ref, send_two_ref, sum_ref = rest
        for i in range(len(rights)):
            at = slice(edges[i], edges[i + 1])
            sum_ref[:, at] = (product(i) + got_ref[0, :, at].astype(F32)).astype(BF)
        if n > edges[-1]:
            sum_ref[:, edges[-1] :] = jnp.zeros((m, n - edges[-1]), BF)

        for ref, rows, wanted in (
            (one_ref, slice(0, part), step % 2 == 0),
            (send_one_ref, slice(0, part), step % 2 == 1),
            (two_ref, slice(part, m), step // 2 == 0),
            (send_two_ref, slice(part, m), step // 2 == 1),
        ):

            @pl.when(wanted)
            def _(ref=ref, rows=rows):
                ref[0] = sum_ref[rows, :]

    place = jnp.stack([side, lax.axis_index("gy")]).astype(jnp.int32)
    in_specs = [ORDER_SPEC] + [
        pl.BlockSpec((size_gx, 1) + x.shape[2:], lambda i, p: (0, p[0], 0, 0)) for x in lefts
    ] + [pl.BlockSpec((1,) + x.shape[1:], lambda i, p: (i ^ p[1], 0, 0)) for x in rights]
    operands = [order.token, *lefts, *rights]
    scratch = []
    if got is None:
        shapes = [jax.ShapeDtypeStruct((4, m, n), BF)]
        out_specs = [pl.BlockSpec((1, m, n), lambda i, p: (i, 0, 0))]
    else:
        operands.append(got)
        in_specs.append(pl.BlockSpec((1, m, n), lambda i, p: (i, 0, 0)))
        shapes = [jax.ShapeDtypeStruct((2, part, n), BF)] * 4
        out_specs = [
            pl.BlockSpec((1, part, n), lambda i, p: (i // 2, 0, 0)),
            pl.BlockSpec((1, part, n), lambda i, p: (i // 2, 0, 0)),
            pl.BlockSpec((1, part, n), lambda i, p: (jnp.minimum(i, 1), 0, 0)),
            pl.BlockSpec((1, part, n), lambda i, p: (jnp.maximum(i, 2) - 2, 0, 0)),
        ]
        scratch = [pltpu.VMEM((m, n), BF)]
    flops = sum(8 * m * x.shape[1] * x.shape[2] for x in rights)
    moved = 8 * m * n * (1 if got is None else 2) + sum(2 * x.size for x in rights)
    order.token, *results = pl.pallas_call(
        kernel,
        out_shape=[ORDER_SHAPE, *shapes],
        grid_spec=pltpu.PrefetchScalarGridSpec(
            num_scalar_prefetch=1,
            grid=(4,),
            in_specs=in_specs,
            out_specs=[ORDER_SPEC, *out_specs],
            scratch_shapes=scratch,
        ),
        cost_estimate=pl.CostEstimate(flops=flops, transcendentals=0, bytes_accessed=moved),
        name="weight_grads_near",
    )(place, *operands)
    return results[0] if got is None else results


def project_back(order, xs, weight, terms, init=None, own=None):
    weight, (w_cols, part) = weight if isinstance(weight, tuple) else (weight, (weight.shape[2], 0))
    width = weight.shape[1]
    rows = xs[0].shape[1] if init is None else init.shape[0]
    rows = max([rows] + [x.shape[1] for x in xs])
    windows = []
    for x, start in zip(xs, terms):
        low = start // 128 * 128
        windows.append((low, min(-(-(start + x.shape[2]) // 128) * 128, w_cols), start - low))
    padded = [w[1] - w[0] != x.shape[2] for x, w in zip(xs, windows)]
    whole = [] if init is None else [init]

    def kernel(*refs):
        refs = list(refs)
        init_ref = refs.pop(0) if whole else None
        x_refs, w_ref = refs[: len(xs)], refs[len(xs)]
        refs = refs[len(xs) + 1 :]
        low_ref = refs.pop(0) if own is not None else None
        out_ref, wide_refs = refs[0], refs[1:]

        @pl.when(pl.program_id(0) == 0)
        def _():
            out_ref[...] = jnp.zeros((rows, width), F32) if init_ref is None else init_ref[...]
            for ref in wide_refs:
                ref[...] = jnp.zeros(ref.shape, BF)

        parts, wide = {}, 0
        for x_ref, (low, high, shift), pad in zip(x_refs, windows, padded):
            r, n = x_ref.shape[1:]
            if pad:
                ref = wide_refs[wide]
                wide += 1
                ref[:, shift : shift + n] = x_ref[0]
                x = ref[...]
            else:
                x = x_ref[0]
            part = dot_t(x, w_ref[0, :, low:high])
            parts[r] = parts[r] + part if r in parts else part
        for r, part in parts.items():
            out_ref[:r] += part
        if low_ref is not None:

            @pl.when(pl.program_id(0) == pl.num_programs(0) - 1)
            def _():
                low_ref[...] = out_ref[own:].astype(BF)

    scratch = [
        pltpu.VMEM((x.shape[1], w[1] - w[0]), BF) for x, w, pad in zip(xs, windows, padded) if pad
    ]
    flops = sum(2 * x.shape[1] * width * x.shape[2] for x in xs)
    wholes = [] if own is None else [((rows - own, width), BF)]
    wholes.append(((rows, width), F32))
    results = by_group(
        order,
        kernel,
        "project_back",
        whole,
        [*xs, (weight, (w_cols, part))],
        [],
        flops,
        wholes,
        scratch,
    )
    return results[0] if own is None else results


def project_qkv(order, hidden, rows, weight, bias_q, bias_v):
    ctx, width = hidden.shape
    n = bias_q.shape[2]

    def kernel(h_ref, w_ref, bq_ref, bv_ref, q_ref, k_ref, v_ref):
        joint = dot_n(h_ref[...], w_ref[0, :, : 3 * n])
        q_ref[0] = (joint[:rows, :n] + bq_ref[0]).astype(BF)
        k_ref[0] = joint[:, n : 2 * n].astype(BF)
        v_ref[0] = (joint[:, 2 * n :] + bv_ref[0]).astype(BF)

    return by_group(
        order,
        kernel,
        "project_qkv",
        [hidden],
        [weight, bias_q, bias_v],
        [((rows, n), BF), ((ctx, n), BF), ((ctx, n), BF)],
        6 * ctx * width * n,
    )


def project_up(order, hidden, weight, bias):
    rows, width = hidden.shape
    n = bias.shape[2]

    def kernel(h_ref, w_ref, bias_ref, act_ref, slope_ref):
        activ, slope = gelu_parts(dot_n(h_ref[...], w_ref[0]) + bias_ref[0])
        act_ref[0] = activ.astype(BF)
        slope_ref[0] = slope.astype(BF)

    return by_group(
        order,
        kernel,
        "project_up",
        [hidden],
        [weight, bias],
        [((rows, n), BF), ((rows, n), BF)],
        2 * rows * width * n,
    )


def project_act_back(order, grad_mlp, weight, slope):
    rows, width = grad_mlp.shape
    n = slope.shape[2]

    def kernel(g_ref, w_ref, slope_ref, low_ref, sums_ref):
        grad = dot_n(g_ref[...], w_ref[0]) * slope_ref[0].astype(F32)
        low_ref[0] = grad.astype(BF)
        sums_ref[0] = jnp.sum(grad, axis=0, keepdims=True)

    return by_group(
        order,
        kernel,
        "project_act_back",
        [grad_mlp],
        [weight, slope],
        [((rows, n), BF), ((1, n), F32)],
        2 * rows * width * n,
    )


def project_mixed_back(order, grad_attn, weight, n, skip):
    rows, width = grad_attn.shape

    def kernel(g_ref, w_ref, out_ref):
        out_ref[0] = dot_n(g_ref[...], w_ref[0])[:, skip:].astype(BF)

    return by_group(
        order,
        kernel,
        "project_mixed_back",
        [grad_attn],
        [weight],
        [((rows, n), BF)],
        2 * rows * width * n,
    )[0]


def head_of(ref, h):
    return ref[0, :, h * HD : (h + 1) * HD]


def attend(order, queries, keys_ctx, values_ctx):
    _, rows, n = queries.shape
    ctx = keys_ctx.shape[1]
    heads = n // HD

    def kernel(q_ref, k_ref, v_ref, mixed_ref, sums_ref, tops_ref):
        for h in range(heads):
            q, k, v = head_of(q_ref, h), head_of(k_ref, h), head_of(v_ref, h)
            scores = dot_t(k, q)
            top = jnp.max(scores, axis=0, keepdims=True)
            weights = jnp.exp2((scores - top) * (SCALE * LOG2E))
            total = jnp.sum(weights, axis=0, keepdims=True)
            mixed = dot_n(v.T, weights.astype(BF)) / total
            mixed_ref[0, :, h * HD : (h + 1) * HD] = mixed.T.astype(BF)
            sums_ref[0, h : h + 1, :] = top * (SCALE * LOG2E) + jnp.log2(total)
            tops_ref[0, h : h + 1, :] = top * SCALE

    return by_group(
        order,
        kernel,
        "attend",
        [],
        [queries, keys_ctx, values_ctx],
        [((rows, n), BF), ((heads, rows), F32), ((heads, rows), F32)],
        14 * rows * ctx * n,
    )


def attend_back(order, queries, keys_ctx, values_ctx, mixed, grad_mixed, log_sums, heads):
    _, rows, n = queries.shape
    ctx = keys_ctx.shape[1]
    n_out = len(heads) * HD

    def kernel(q_ref, k_ref, v_ref, x_ref, g_ref, sums_ref, gq_ref, gk_ref, gv_ref):
        for j, h in enumerate(heads):
            q, k, v = head_of(q_ref, h), head_of(k_ref, h), head_of(v_ref, h)
            grad = head_of(g_ref, h)
            delta = jnp.sum(
                (head_of(x_ref, h).astype(F32) * grad.astype(F32)).T, axis=0, keepdims=True
            )
            probs = jnp.exp2(dot_t(k, q) * (SCALE * LOG2E) - sums_ref[0, h : h + 1, :])
            grad_scores = (probs * (dot_t(v, grad) - delta)).astype(BF)
            out = slice(j * HD, (j + 1) * HD)
            gk_ref[0, :, out] = (dot_n(grad_scores, q) * SCALE).astype(BF)
            gv_ref[0, :, out] = dot_n(probs.astype(BF), grad).astype(BF)
            gq_ref[0, :, out] = (dot_n(k.T, grad_scores) * SCALE).T.astype(BF)

    return by_group(
        order,
        kernel,
        "attend_back",
        [],
        [queries, keys_ctx, values_ctx, mixed, grad_mixed, log_sums],
        [((rows, n_out), BF), ((ctx, n_out), BF), ((ctx, n_out), BF)],
        35 * rows * ctx * n_out,
    )


def body(
    latents_in,
    condition,
    ada_weight,
    ada_bias,
    query_weight,
    key_weight,
    value_weight,
    query_bias,
    value_bias,
    out_weight,
    out_bias,
    up_weight,
    up_bias,
    down_weight,
    down_bias,
    grad_out,
):
    rows, width = latents_in.shape
    latent_count = condition.shape[0]
    cols = query_weight.shape[1]
    width_x = out_bias.shape[0]
    size_gx, size_gy = lax.axis_size("gx"), lax.axis_size("gy")
    at_gx, at_gy = lax.axis_index("gx"), lax.axis_index("gy")
    span = SEQ // rows
    heads_here = cols // HD

    def rows_sum(values):
        return jnp.sum(values, axis=-2).reshape(-1, width)

    def shift_pairs(shift):
        return [(i, i // span * span + (i + shift) % span) for i in range(size_gx)]

    context = jnp.concatenate(
        [latents_in] + [lax.ppermute(latents_in, "gx", shift_pairs(s)) for s in range(1, span)], axis=0
    )

    cond_f32 = condition.astype(F32)
    silu_cond = jax.nn.silu(cond_f32).astype(BF)
    mod_part = dot("le,emf->lmf", silu_cond, ada_weight)
    for bit in reversed(bits_of("gy")):
        mod_pair = mod_part.reshape((2, -1) + mod_part.shape[1:])
        side = (at_gy // bit) % 2
        mod_part = pick(mod_pair, side) + swap(pick(mod_pair, 1 - side), "gy", bit)
    mod_own = pick(mod_part, at_gx // span) + ada_bias
    shift_one, scale_one, gate_one, shift_two, scale_two, gate_two = [
        mod_own[m : m + 1] for m in range(6)
    ]

    along_x = cube_gather(jnp.concatenate([out_bias, down_bias])[None], "gx")
    out_bias_all = along_x[:, :width_x].reshape(1, width)
    down_bias_all = along_x[:, width_x:].reshape(1, width)
    rest = cube_gather(jnp.concatenate([query_bias, value_bias, up_bias])[None], "gy")
    query_bias_all = rest[:, None, :cols]
    value_bias_all = rest[:, None, cols : 2 * cols]
    up_bias_all = rest[:, None, 2 * cols :]

    order = Order()
    up_cols = up_bias.shape[0]
    attn_part = jnp.concatenate([query_weight, key_weight, value_weight, out_weight.T], axis=1)
    if up_cols == 4 * cols and up_cols % 128 == 0:
        joint_w = gather_weight(jnp.concatenate([attn_part, up_weight], axis=1))
        attn_w, up_w = (joint_w, (up_cols, 0)), (joint_w, (up_cols, 1))
    else:
        attn_w = (gather_weight(attn_part), (4 * cols, 0))
        up_w = (gather_weight(up_weight), (up_cols, 0))
    out_start = 3 * cols // 128 * 128
    out_width = 4 * cols - out_start
    if out_width % 128 or out_start % out_width:
        out_start, out_width = 0, 4 * cols
    out_w = (attn_w[0], (out_width, out_start // out_width))
    out_skip = 3 * cols - out_start
    down_w = gather_weight(down_weight.T)
    grad_mlp = gate_two * grad_out
    grad_mlp_low = grad_mlp.astype(BF)

    normed_ctx, inverse_ctx = normalize(context.astype(F32))
    hidden_ctx = (normed_ctx * (1.0 + scale_one) + shift_one).astype(BF)
    normed_one, inverse_one, hidden_one = normed_ctx[:rows], inverse_ctx[:rows], hidden_ctx[:rows]
    residual = latents_in.astype(F32)
    hidden_t, grad_mlp_t = transposed(order, hidden_ctx, grad_mlp_low)
    queries, keys_ctx, values_ctx = project_qkv(
        order, hidden_ctx, rows, attn_w, query_bias_all, value_bias_all
    )
    mixed, log_sums, head_tops = attend(order, queries, keys_ctx, values_ctx)
    head_tops = jnp.max(head_tops, axis=2)
    attn_out = project_back(order, [mixed], out_w, [out_skip]) + out_bias_all
    after_attn = residual + gate_one * attn_out
    normed_two, inverse_two = normalize(after_attn)
    hidden_two = (normed_two * (1.0 + scale_two) + shift_two).astype(BF)
    activation, gelu_slope = project_up(order, hidden_two, up_w, up_bias_all)
    sum_down = Exchange(scatter_steps(order, [grad_mlp_t], [0], [activation]))
    order.tick(sum_down)
    grad_up_low, up_sums = project_act_back(order, grad_mlp_low, down_w, gelu_slope)
    sum_up = Exchange(scatter_steps(order, [hidden_two.T], [0], [grad_up_low]))
    grad_hidden_two = project_back(order, [grad_up_low], up_w, [0])
    mlp_out = project_back(order, [activation], down_w, [0]) + down_bias_all
    order.tick(sum_down, sum_up)
    block_out = after_attn + gate_two * mlp_out
    grad_after = grad_out + normalize_back(
        grad_hidden_two * (1.0 + scale_two), normed_two, inverse_two
    )
    grad_attn = gate_one * grad_after
    grad_attn_low = grad_attn.astype(BF)
    grad_mixed_low = project_mixed_back(order, grad_attn_low, out_w, cols, out_skip)
    grad_attn_t = grad_attn_low.T
    tops_row = jnp.zeros((1, width), F32).at[0, : size_gy * heads_here].set(head_tops.reshape(-1))
    early = Exchange(
        total_steps(
            jnp.concatenate(
                [rows_sum(grad_mlp), rows_sum(grad_attn), up_sums.reshape(-1, width), tops_row],
                axis=0,
            )
        )
    )

    half = (heads_here + 1) // 2
    head_sets = [x for x in (range(half), range(half, heads_here)) if len(x)]
    sum_attn, back_parts, grad_ctx = [], [], None
    grad_low = None
    for i, heads in enumerate(head_sets):
        parts = attend_back(
            order, queries, keys_ctx, values_ctx, mixed, grad_mixed_low, log_sums, heads
        )
        back_parts.append(parts)
        extra, last = i == 0, i + 1 == len(head_sets)
        sum_new = Exchange(
            scatter_steps(
                order,
                [hidden_t] + [grad_attn_t] * extra,
                [0, 0, 0] + [1] * extra,
                list(parts) + [mixed] * extra,
            )
        )
        order.tick(early, sum_down, sum_up, *sum_attn)
        sum_attn.append(sum_new)
        start = heads[0] * HD
        grad_ctx = project_back(
            order,
            list(parts),
            attn_w,
            [start, cols + start, 2 * cols + start],
            grad_ctx,
            rows if last and span > 1 else None,
        )
        if last and span > 1:
            grad_low, grad_ctx = grad_ctx
        order.tick(early, sum_down, sum_up, *sum_attn)
    grad_hidden_one = grad_ctx[:rows]
    if span == 2:
        pairs = [[i, i + 1] for i in range(0, size_gx, 2)]
        both = lax.all_gather(grad_low, "gx", axis=0, axis_index_groups=pairs)
        order.token, both = lax.optimization_barrier((order.token, both))
        backs = [pick(both, 1 - at_gx % 2)]
    else:
        backs = [
            lax.ppermute(
                grad_low[(s - 1) * rows : s * rows], "gx", [(b, a) for a, b in shift_pairs(s)]
            )
            for s in range(1, span)
        ]
    for back in backs:
        grad_hidden_one += back.astype(F32)
    grad_input = grad_after + normalize_back(
        grad_hidden_one * (1.0 + scale_one), normed_one, inverse_one
    )

    def group_sum(i):
        return jnp.concatenate(
            [jnp.sum(x[i].astype(F32), axis=1) for x in back_parts], axis=1
        ).reshape(1, width)

    late = jnp.concatenate(
        [
            rows_sum(grad_hidden_one),
            rows_sum(grad_hidden_one * normed_one),
            rows_sum(grad_after * attn_out),
            rows_sum(grad_hidden_two),
            rows_sum(grad_hidden_two * normed_two),
            rows_sum(grad_out * mlp_out),
            group_sum(0),
            group_sum(2),
        ],
        axis=0,
    )
    late += order.token[:1, :1]
    for bit in bits_of("gx"):
        if bit < span:
            late = late + swap(late, "gx", bit)
    late = late.astype(BF)[None]
    for axis in ("gx", "gy"):
        for bit in bits_of(axis):
            if axis == "gy" or bit >= span:
                late = jnp.concatenate([late, swap(late, axis, bit)], axis=0)
    late_all = jnp.concatenate([late, swap(late, "dp", 1)], axis=0)
    at_latent = at_gy * (size_gx // span) + at_gx // span
    grad_ada_b = jnp.sum(late_all[:, :6].astype(F32), axis=0)
    tail_sum = jnp.sum(late_all[:, 6:].astype(F32), axis=0)
    grad_query_b = lax.dynamic_slice_in_dim(tail_sum[0], at_gy * cols, cols, 0)
    grad_value_b = lax.dynamic_slice_in_dim(tail_sum[1], at_gy * cols, cols, 0)
    silu_near = by_distance(silu_cond, at_latent)
    silu_every = jnp.concatenate(
        [silu_near, by_distance(swap(silu_cond, "dp", 1), at_latent)], axis=0
    )
    grad_ada_w = dot("le,lmf->emf", silu_every, late_all[:, :6])
    grad_silu = by_distance(dot("lmf,emf->le", late[:, :6], ada_weight), at_latent)
    sigmoid_cond = jax.nn.sigmoid(cond_f32)
    grad_condition = grad_silu * sigmoid_cond * (1.0 + cond_f32 * (1.0 - sigmoid_cond))

    early_sum = early.result()
    grad_down_b = lax.dynamic_slice_in_dim(early_sum[0], at_gx * width_x, width_x, 0)
    grad_out_b = lax.dynamic_slice_in_dim(early_sum[1], at_gx * width_x, width_x, 0)
    grad_up_b = lax.dynamic_slice_in_dim(early_sum[2:-1].reshape(-1), at_gy * up_cols, up_cols, 0)
    logit_max = lax.dynamic_slice_in_dim(early_sum[-1], at_gy * heads_here, heads_here, 0)

    grad_down_w, grad_up_w = sum_down.result(), sum_up.result()
    sums = [x.result() for x in sum_attn]
    grad_qkv = [
        jnp.concatenate(
            [x[:, i * HD * len(h) : (i + 1) * HD * len(h)] for x, h in zip(sums, head_sets)], axis=1
        )
        for i in range(3)
    ]
    out_at = 3 * HD * len(head_sets[0])
    grad_out_w = sums[0][:, out_at : out_at + cols]

    factor = TAU / jnp.maximum(logit_max, TAU)
    root_cols = jnp.repeat(jnp.sqrt(factor), HD)
    clipped_query = query_weight.astype(F32) * root_cols[None, :]
    clipped_key = key_weight.astype(F32) * root_cols[None, :]
    clipped_bias = query_bias * root_cols
    return (
        block_out,
        grad_input,
        grad_condition,
        grad_ada_w,
        grad_ada_b,
        *grad_qkv,
        grad_query_b,
        grad_value_b,
        grad_out_w.T,
        grad_out_b,
        grad_up_w,
        grad_up_b,
        grad_down_w.T,
        grad_down_b,
        logit_max,
        clipped_query,
        clipped_key,
        clipped_bias,
    )


def solution(mesh):
    placed = (
        P(("dp", "gy", "gx"), None),
        P("dp", "gy"),
        P("gy", None, None),
        P(),
        P("gx", "gy"),
        P("gx", "gy"),
        P("gx", "gy"),
        P("gy"),
        P("gy"),
        P("gy", "gx"),
        P("gx"),
        P("gx", "gy"),
        P("gy"),
        P("gy", "gx"),
        P("gx"),
        P(("dp", "gy", "gx"), None),
    )
    return jax.shard_map(
        body,
        mesh=mesh,
        in_specs=placed,
        out_specs=(
            P(("dp", "gy", "gx"), None),
            P(("dp", "gy", "gx"), None),
            P("dp", "gy"),
            P("gy", None, None),
            P(),
            P("gx", "gy"),
            P("gx", "gy"),
            P("gx", "gy"),
            P("gy"),
            P("gy"),
            P("gy", "gx"),
            P("gx"),
            P("gx", "gy"),
            P("gy"),
            P("gy", "gx"),
            P("gx"),
            P("gy"),
            P("gx", "gy"),
            P("gx", "gy"),
            P("gy"),
        ),
        check_vma=False,
    )
```
